32 devices in a mesh: fiber: 2 (over y), gx: 8 (over z, x), gy: 2 (over core).
Axes of the slice: x: 2, y: 2, z: 4, core: 2. Of those that a mesh axis runs over, the one named last changes fastest.
Arguments:
- optical_phase: bfloat16 [3072, 1024], P(('fiber', 'gx'), 'gy'), parts along dimension 0, may hold values from -6 to 6
- gauge_length: int32 [8], P('fiber'), parts along dimension 0, may hold values from 8 to 16, as said below
- snap_starts: int32 [32], P(('fiber', 'gx')), parts along dimension 0, may hold values from 0 to 64, as said below
- partner_offsets: int32 [8, 2], P('fiber'), parts along dimension 0, may hold values from -3 to 3, as said below
Outputs:
- gram_tiles: bfloat16 [4, 256, 4, 2, 256, 256], P('fiber', ('gx', 'gy')), parts along dimension 0
The draws below stay inside these ranges and needn't reach their ends.
There are 2 independent parts, one for each index of `fiber`. The reference program is written for one: setup_inputs(seed, part) draws one part's arguments, and reference() takes and returns one part's arrays. A program takes and returns all parts, laid end to end along the dimension named above; each array names one. Nothing has to cross between parts.
Inputs may be any that keep to these rules, and one draw needn't show every extreme that they name: `gauge_length`: some block uses exactly 16. Snapshot s starts at sample (s // 2) * 192 + snap_starts[s] of the window and lies within that stretch of 192 samples; some snapshot has start 0 and some has 64. `partner_offsets`: block b's partners b + offset lie inside the fiber and differ from b; block 0 has the last block as a partner and the last block has block 0.
All inputs are finite; a program needn't handle non-finite values.
Results may differ from the reference program's by a relative error of at most 0.007.
Values may be sent and summed in bfloat16 or wider, within the bound.
No kernel may reach another device: no remote copies, remote signals or barrier semaphores. Data moves between devices by JAX's collectives and lax.ppermute only.
A program may use at most 128 MiB of HBM per device.

```python
import math
import jax
import jax.numpy as jnp
from jax import lax

BINS = 256
BLOCK = 256
SNAP_LEN = 128
GAUGE_MAX = 16
PARTNERS = 2
TIME_DEV = 192
SNAP_DEV = 2
CHANNELS = 1024
BLOCKS = 4
SNAPS = 16
TIME_ALL = 1536


def draw_gauge_length(key, part):
    inner = jax.random.fold_in(key, 11)
    value_key, place_key = jax.random.split(inner)
    values = jax.random.randint(value_key, (BLOCKS,), GAUGE_MAX // 2, GAUGE_MAX + 1, dtype=jnp.int32)
    chosen = jax.random.randint(place_key, (), 0, BLOCKS, dtype=jnp.int32)
    places = jnp.arange(BLOCKS, dtype=jnp.int32)
    return jnp.where(places == chosen, GAUGE_MAX, values).astype(jnp.int32)


def draw_snap_starts(key, part):
    inner = jax.random.fold_in(key, 23)
    value_key, high_key, low_key = jax.random.split(inner, 3)
    values = jax.random.randint(value_key, (SNAPS,), 0, TIME_DEV - SNAP_LEN + 1, dtype=jnp.int32)
    high_at = jax.random.randint(high_key, (), 0, SNAPS, dtype=jnp.int32)
    low_at = (high_at + 1 + jax.random.randint(low_key, (), 0, SNAPS - 1, dtype=jnp.int32)) % SNAPS
    places = jnp.arange(SNAPS, dtype=jnp.int32)
    values = jnp.where(places == high_at, TIME_DEV - SNAP_LEN, values)
    values = jnp.where(places == low_at, 0, values)
    return values.astype(jnp.int32)


def draw_partner_offsets(key, part):
    inner = jax.random.fold_in(key, 37)
    jumps = jax.random.randint(inner, (BLOCKS, PARTNERS), 1, BLOCKS, dtype=jnp.int32)
    own_block = jnp.arange(BLOCKS, dtype=jnp.int32)[:, None]
    partner = (own_block + jumps) % BLOCKS
    column_id = jnp.arange(PARTNERS, dtype=jnp.int32)[None, :]
    partner = jnp.where((own_block == 0) & (column_id == 0), BLOCKS - 1, partner)
    partner = jnp.where((own_block == BLOCKS - 1) & (column_id == 0), 0, partner)
    return (partner - own_block).astype(jnp.int32)


def shard_levels(key, extent, shards, smallest, largest):
    factor_of, own = 1.0, jax.random.fold_in(key, 6)
    for dim, parts in shards:
        heights = jnp.exp(jax.random.uniform(jax.random.fold_in(own, dim), (parts,), jnp.float32, smallest / len(shards), largest / len(shards)))
        factor_of = factor_of * jnp.repeat(heights, extent[dim] // parts).reshape([-1 if axis == dim else 1 for axis in range(len(extent))])
    return factor_of


def gaussian(own_key, extent, scale, reach, cuts=(), held_as=jnp.bfloat16):
    entries = scale * jax.random.normal(own_key, extent, jnp.float32)
    if cuts:
        entries = entries * shard_levels(own_key, extent, cuts, -0.22, 0.18)
    return jnp.clip(entries, -reach, reach).astype(held_as)


def setup_inputs(seed: int = 0, part: int = 0) -> dict:
    splits = jax.random.split(jax.random.key(seed), 5)
    own_keys = jax.random.split(jax.random.fold_in(splits[4], part), 5)
    optical_phase = gaussian(own_keys[0], (TIME_ALL, CHANNELS), 1.0, 6.0, ((0, 8), (1, 2)))
    gauge_length = draw_gauge_length(jax.random.fold_in(jax.random.fold_in(splits[4], part), 71), part)
    snap_starts = draw_snap_starts(jax.random.fold_in(jax.random.fold_in(splits[4], part), 71), part)
    partner_offsets = draw_partner_offsets(jax.random.fold_in(jax.random.fold_in(splits[4], part), 71), part)
    return dict(optical_phase=optical_phase, gauge_length=gauge_length, snap_starts=snap_starts, partner_offsets=partner_offsets)


def fourier_table(bin_index, total_len):
    sample = jnp.arange(SNAP_LEN, dtype=jnp.int32)
    product = bin_index[:, None] * sample[None, :] % total_len
    angles = 2.0 * math.pi / total_len * product.astype(jnp.float32)
    factor = 1.0 / math.sqrt(SNAP_LEN)
    return jnp.stack([jnp.cos(angles) * factor, -jnp.sin(angles) * factor]).astype(jnp.bfloat16)

def taper_window():
    sample = jnp.arange(SNAP_LEN, dtype=jnp.int32).astype(jnp.float32)
    return 0.5 - 0.5 * jnp.cos(2.0 * math.pi / SNAP_LEN * sample)

def strain_blocks(extended, gauges):
    blocks = gauges.shape[0]
    block_first = jnp.arange(blocks, dtype=jnp.int32) * BLOCK

    def pick_block(column):
        return lax.dynamic_slice_in_dim(extended, column, BLOCK, 1)
    shifted = jax.vmap(pick_block)(block_first + gauges)
    initial = extended[:, :blocks * BLOCK].reshape(extended.shape[0], blocks, BLOCK)
    return shifted - jnp.transpose(initial, (1, 0, 2))

def reference(optical_phase, gauge_length, snap_starts, partner_offsets):
    wide_phase = optical_phase.astype(jnp.float32)
    rows_total = wide_phase.shape[0]
    edge_cols = jnp.broadcast_to(wide_phase[:, -1:], (rows_total, GAUGE_MAX))
    extended = jnp.concatenate([wide_phase, edge_cols], axis=1)
    strain = strain_blocks(extended, gauge_length)
    absolute = jnp.arange(SNAPS, dtype=jnp.int32) // SNAP_DEV * TIME_DEV + snap_starts
    fourier = fourier_table(jnp.arange(BINS, dtype=jnp.int32), 2 * BINS).astype(jnp.float32)
    window = taper_window()

    def one_snapshot(row_start):
        segment = lax.dynamic_slice_in_dim(strain, row_start, SNAP_LEN, 1)
        rounded = lax.optimization_barrier((window[None, :, None] * segment).astype(jnp.bfloat16))
        tapered = rounded.astype(jnp.float32)
        spectrum = jnp.einsum('cft,btj->cfbj', fourier, tapered, precision=lax.Precision.HIGHEST)
        return spectrum.astype(jnp.bfloat16)
    spectra = lax.map(one_snapshot, absolute)
    partners = jnp.arange(BLOCKS, dtype=jnp.int32)[:, None] + partner_offsets
    norm_scale = 1.0 / math.sqrt(SNAPS)

    def one_bin(bin_id):
        column = lax.dynamic_index_in_dim(spectra, bin_id, 2, keepdims=False)
        partner_data = jnp.take(column, partners.reshape(-1), axis=2).reshape(SNAPS, 2, BLOCKS, PARTNERS, BLOCK)
        swapped = jnp.stack([partner_data[:, 1], -partner_data[:, 0]], axis=1)
        stacked = jnp.stack([partner_data, swapped]).astype(jnp.float32)
        gram_tile = jnp.einsum('scbi,pscbkj->pbkij', column.astype(jnp.float32), stacked, precision=lax.Precision.HIGHEST)
        return (gram_tile * norm_scale).astype(jnp.bfloat16)
    all_tiles = lax.map(one_bin, jnp.arange(BINS, dtype=jnp.int32))
    return jnp.transpose(all_tiles, (1, 0, 2, 3, 4, 5))
```

```python
import functools
import math

import jax
import jax.numpy as jnp
from jax import lax
from jax.experimental import pallas as pl
from jax.experimental.pallas import tpu as pltpu
from jax.sharding import PartitionSpec as P

BINS = 256
BLOCK = 256
SNAP_LEN = 128
GAUGE_MAX = 16
PARTNERS = 2
LANES = 128


def fourier_table(bin_index, total_len):
    sample = jnp.arange(SNAP_LEN, dtype=jnp.int32)
    product = bin_index[:, None] * sample[None, :] % total_len
    angles = 2.0 * math.pi / total_len * product.astype(jnp.float32)
    factor = 1.0 / math.sqrt(SNAP_LEN)
    return jnp.stack([jnp.cos(angles) * factor, -jnp.sin(angles) * factor]).astype(jnp.bfloat16)


def taper_window():
    sample = jnp.arange(SNAP_LEN, dtype=jnp.int32).astype(jnp.float32)
    return 0.5 - 0.5 * jnp.cos(2.0 * math.pi / SNAP_LEN * sample)


def ring_order(count):
    return [*range(0, count, 2), *range(count - 1, 0, -2)]


def taper_stretch(ext_ref, strain_ref, tap_ref, row, own_ref, sib_ref, gauge, start_of, window, side):
    half = own_ref[0].shape[1]
    at = 0
    for own, sib in zip(own_ref, sib_ref, strict=True):
        rows = pl.ds(at, own.shape[0])
        at += own.shape[0]
        ext_ref[rows, pl.ds(pl.multiple_of(side * half, half), half)] = own[...].astype(jnp.float32)
        ext_ref[rows, pl.ds(pl.multiple_of((1 - side) * half, half), half)] = sib[...].astype(jnp.float32)
    width = 2 * half
    rows_all = ext_ref.shape[0]
    reach = SNAP_LEN + 8
    ext_ref[:, width : width + LANES] = jnp.broadcast_to(ext_ref[:, width - 1 : width], (rows_all, LANES))
    span = BLOCK + LANES
    for blk in range(width // BLOCK):
        wide = ext_ref[:, blk * BLOCK : blk * BLOCK + span]
        moved = pltpu.roll(wide, span - gauge(blk), 1)[:, :BLOCK]
        strain_ref[:rows_all, blk * BLOCK : (blk + 1) * BLOCK] = moved - wide[:, :BLOCK]
    for snap in range(2):
        start = start_of(snap)
        odd = lax.rem(start, 8)
        base = pl.ds(pl.multiple_of(start - odd, 8), reach)
        for tile in range(width // LANES):
            cols = slice(tile * LANES, (tile + 1) * LANES)
            seg = pltpu.roll(strain_ref[base, cols], lax.rem(reach - odd, reach), 0)[:SNAP_LEN]
            tap_ref[row + snap * SNAP_LEN : row + (snap + 1) * SNAP_LEN, cols] = (window * seg).astype(jnp.bfloat16)


def spectra_kernel(count, gauge_ref, starts_ref, table_ref, window_ref, *refs):
    own, sib = refs[:count], refs[count : 2 * count]
    out_ref, ext_ref, strain_ref, tap_ref = refs[2 * count :]
    side = lax.axis_index("gy")
    for n in range(count):
        taper_stretch(
            ext_ref, strain_ref, tap_ref, n * 2 * SNAP_LEN, (own[n],), (sib[n],), lambda blk: gauge_ref[blk],
            lambda snap, n=n: starts_ref[2 * n + snap], window_ref[...], side,
        )
    spectrum = jnp.dot(
        table_ref[:, : count * 2 * SNAP_LEN], tap_ref[...], preferred_element_type=jnp.float32
    )
    out_ref[...] = spectrum.reshape(out_ref.shape)


def spectra_group(gauge, starts, table, window, own, sib):
    count = len(own)
    rows, half = own[0].shape
    bins = table.shape[0] // 16
    vmem, smem = pl.BlockSpec(memory_space=pltpu.VMEM), pl.BlockSpec(memory_space=pltpu.SMEM)
    return pl.pallas_call(
        functools.partial(spectra_kernel, count),
        in_specs=[smem, smem] + [vmem] * (2 + 2 * count),
        out_specs=vmem,
        out_shape=jax.ShapeDtypeStruct((bins, 16, 2 * half), jnp.float32),
        scratch_shapes=[
            pltpu.VMEM((rows, 2 * half + LANES), jnp.float32),
            pltpu.VMEM((rows + 8, 2 * half), jnp.float32),
            pltpu.VMEM((count * 2 * SNAP_LEN, 2 * half), jnp.bfloat16),
        ],
        cost_estimate=pl.CostEstimate(flops=count * 300_000_000, bytes_accessed=count * 400_000, transcendentals=0),
        name="spectra",
    )(gauge, starts, table, window, *own, *sib)


def gram_kernel(
    scale, slots, unroll, gauge_ref, starts_ref, offset_ref, table_ref, window_ref, first_ref, second_ref,
    own0, own1, sib0, sib1, out_ref, ext_ref, strain_ref, tap_ref, last_ref, right_ref, buf_ref, sems,
):
    side = lax.axis_index("gy")
    bins, _, width = first_ref.shape
    blocks = width // BLOCK
    taper_stretch(
        ext_ref, strain_ref, tap_ref, 0, (own0, own1), (sib0, sib1), lambda blk: gauge_ref[blk],
        lambda snap: starts_ref[snap], window_ref[...], side,
    )
    last = jnp.dot(table_ref[:, 3 * 2 * SNAP_LEN :], tap_ref[...], preferred_element_type=jnp.float32)
    last_ref[...] = second_ref[...] + last.reshape(last_ref.shape)

    def copies(f, slot):
        return [
            pltpu.make_async_copy(buf_ref.at[slot, part], out_ref.at[part, f], sems.at[slot, part])
            for part in range(2)
        ]

    def one(f, slot, place):
        pieces = [first_ref[f, :8], first_ref[f, 8:], last_ref[f, :8], last_ref[f, 8:]]
        left = jnp.concatenate(pieces, axis=0).astype(jnp.bfloat16)
        turned = jnp.concatenate([pieces[1], -pieces[0], pieces[3], -pieces[2]], axis=0).astype(jnp.bfloat16)
        for blk in range(blocks):
            right_ref[place, blk, :, :BLOCK] = left[:, blk * BLOCK : (blk + 1) * BLOCK]
            right_ref[place, blk, :, BLOCK:] = turned[:, blk * BLOCK : (blk + 1) * BLOCK]
        for blk in range(blocks):
            for k in range(PARTNERS):
                tile = lax.dot_general(
                    left[:, blk * BLOCK : (blk + 1) * BLOCK],
                    right_ref[place, blk + offset_ref[blk, k]],
                    (((0,), (0,)), ((), ())),
                    preferred_element_type=jnp.float32,
                )
                if scale != 1.0:
                    tile = tile * scale
                buf_ref[slot, 0, blk, k] = tile[:, :BLOCK].astype(jnp.bfloat16)
                buf_ref[slot, 1, blk, k] = tile[:, BLOCK:].astype(jnp.bfloat16)
        for c in copies(f, slot):
            c.start()

    def step(i, carry):
        for u in range(unroll):
            f = i * unroll + u

            @pl.when(f >= slots)
            def _(f=f):
                for c in copies(f - slots, lax.rem(f, slots)):
                    c.wait()

        for u in range(unroll):
            f = i * unroll + u
            one(f, lax.rem(f, slots), u)
        return carry

    lax.fori_loop(0, bins // unroll, step, 0)
    for f in range(bins - slots, bins):
        for c in copies(f, f % slots):
            c.wait()


def gram(scale, gauge, starts, offsets, table, window, first, second, own, sib):
    bins, _, width = first.shape
    blocks = width // BLOCK
    rows = sum(piece.shape[0] for piece in own)
    slots, unroll = 4, 2
    vmem, smem = pl.BlockSpec(memory_space=pltpu.VMEM), pl.BlockSpec(memory_space=pltpu.SMEM)
    return pl.pallas_call(
        functools.partial(gram_kernel, scale, slots, unroll),
        in_specs=[smem] * 3 + [vmem] * 8,
        out_specs=pl.BlockSpec(memory_space=pltpu.HBM),
        out_shape=jax.ShapeDtypeStruct((2, bins, blocks, PARTNERS, BLOCK, BLOCK), jnp.bfloat16),
        scratch_shapes=[
            pltpu.VMEM((rows, width + LANES), jnp.float32),
            pltpu.VMEM((rows + 8, width), jnp.float32),
            pltpu.VMEM((2 * SNAP_LEN, width), jnp.bfloat16),
            pltpu.VMEM(second.shape, jnp.float32),
            pltpu.VMEM((unroll, blocks, 32, 2 * BLOCK), jnp.bfloat16),
            pltpu.VMEM((slots, 2, blocks, PARTNERS, BLOCK, BLOCK), jnp.bfloat16),
            pltpu.SemaphoreType.DMA((slots, 2)),
        ],
        name="gram",
    )(gauge, starts, offsets, table, window, first, second, *own, *sib)


def on_device_ring(optical_phase, gauge_length, snap_starts, partner_offsets):
    count = lax.axis_size("gx")
    pair_devices = lax.axis_size("gy")
    rows_local = optical_phase.shape[0]
    bins_dev = BINS // (count * pair_devices)
    snaps_all = count * snap_starts.shape[0]
    order = ring_order(count)
    ahead = [(order[i], order[(i + 1) % count]) for i in range(count)]
    back = [(b, a) for a, b in ahead]
    swap = [(0, 1), (1, 0)]

    scale = 1.0 / math.sqrt(snaps_all)
    root = math.sqrt(scale)
    if math.frexp(root)[0] == 0.5:
        fold, scale = root, 1.0
    else:
        fold = 1.0
    bin_index = (lax.axis_index("gx") * pair_devices + lax.axis_index("gy")) * bins_dev + jnp.arange(
        bins_dev, dtype=jnp.int32
    )

    def exchange(x):
        return lax.ppermute(x, "gy", swap)

    def tie(*xs):
        return lax.optimization_barrier(xs)

    half_rows = rows_local // 2
    own, tiny = optical_phase, snap_starts
    f1, b1 = lax.ppermute(own, "gx", ahead), lax.ppermute(own, "gx", back)
    tf1, tb1 = lax.ppermute(tiny, "gx", ahead), lax.ppermute(tiny, "gx", back)
    s_own = exchange(own)
    f1, b1, tf1, tb1 = tie(f1, b1, tf1, tb1)
    f2, b2 = lax.ppermute(f1, "gx", ahead), lax.ppermute(b1, "gx", back)
    tf2, tb2 = lax.ppermute(tf1, "gx", ahead), lax.ppermute(tb1, "gx", back)
    s_f1, s_b1 = exchange(f1), exchange(b1)
    f2, b2, tf2, tb2 = tie(f2, b2, tf2, tb2)
    f3, b3 = lax.ppermute(f2, "gx", ahead), lax.ppermute(b2, "gx", back)
    tf3, tb3 = lax.ppermute(tf2, "gx", ahead), lax.ppermute(tb2, "gx", back)
    s_f2, s_b2 = exchange(f2), exchange(b2)
    f3, b3, tf3, tb3 = tie(f3, b3, tf3, tb3)
    f4, b4 = lax.ppermute(f3[:half_rows], "gx", ahead), lax.ppermute(b3[half_rows:], "gx", back)
    tf4 = lax.ppermute(tf3, "gx", ahead)
    s_f3, s_b3 = exchange(f3), exchange(b3)
    f4, b4 = tie(f4, b4)
    s_f4, s_b4 = exchange(f4), exchange(b4)

    window = jnp.broadcast_to(taper_window()[:, None], (SNAP_LEN, LANES))
    fourier = fourier_table(bin_index, 2 * BINS) * jnp.bfloat16(fold)
    same = jnp.arange(8)[:, None] == jnp.arange(8)[None, :]
    table = jnp.where(
        same[None, None, :, :, None], jnp.transpose(fourier, (1, 0, 2))[:, :, None, None, :], jnp.bfloat16(0)
    ).reshape(bins_dev * 16, 8 * SNAP_LEN)

    starts1 = jnp.concatenate([tiny, tf1, tb1, tf2])
    starts2 = jnp.concatenate([tb2, tf3, tb3])
    first = spectra_group(gauge_length, starts1, table, window, (own, f1, b1, f2), (s_own, s_f1, s_b1, s_f2))
    second = spectra_group(gauge_length, starts2, table, window, (b2, f3, b3), (s_b2, s_f3, s_b3))
    return gram(
        scale, gauge_length, tf4, partner_offsets, table, window, first, second, (f4, b4), (s_f4, s_b4)
    )


def strain_blocks(extended, gauges):
    blocks = gauges.shape[0]
    block_first = jnp.arange(blocks, dtype=jnp.int32) * BLOCK

    def pick_block(column):
        return lax.dynamic_slice_in_dim(extended, column, BLOCK, 1)

    shifted = jax.vmap(pick_block)(block_first + gauges)
    initial = extended[:, : blocks * BLOCK].reshape(extended.shape[0], blocks, BLOCK)
    return shifted - jnp.transpose(initial, (1, 0, 2))


def tapered_segments(strain, start_rows):
    window = taper_window()

    def segment_at(row_start):
        return lax.dynamic_slice_in_dim(strain, row_start, SNAP_LEN, 1)

    segments = jax.vmap(segment_at)(start_rows)
    return (window[None, None, :, None] * segments).astype(jnp.bfloat16)


def spectra_for(tapered, bin_index):
    fourier = fourier_table(bin_index, 2 * BINS)
    spectrum = jnp.einsum("cft,sbtj->scfbj", fourier, tapered, preferred_element_type=jnp.float32)
    shape_out = spectrum.shape
    return spectrum.astype(jnp.bfloat16).reshape(
        shape_out[0], 2, shape_out[2], shape_out[3] * BLOCK
    )


def on_device(optical_phase, gauge_length, snap_starts, partner_offsets):
    time_devices = lax.axis_size("gx")
    pair_devices = lax.axis_size("gy")
    pair_index = lax.axis_index("gy")
    rows_local = optical_phase.shape[0]
    bins_dev = BINS // (time_devices * pair_devices)
    whole_phase = lax.all_gather(optical_phase, "gy", axis=1, tiled=True)
    edge_cols = jnp.broadcast_to(whole_phase[:, -1:], (rows_local, GAUGE_MAX))
    extended = jnp.concatenate([whole_phase, edge_cols], axis=1).astype(jnp.float32)
    strain = strain_blocks(extended, gauge_length)
    tapered = tapered_segments(strain, snap_starts)
    owner_slot = jnp.arange(time_devices * bins_dev, dtype=jnp.int32)
    bin_index = (
        owner_slot // bins_dev * pair_devices + pair_index
    ) * bins_dev + owner_slot % bins_dev
    spectra = spectra_for(tapered, bin_index)
    gathered = lax.all_to_all(spectra, "gx", split_axis=2, concat_axis=0, tiled=True)
    snaps_all = gathered.shape[0]
    blocks_all = gathered.shape[3] // BLOCK
    spectra_blocks = gathered.reshape(snaps_all, 2, bins_dev, blocks_all, BLOCK)
    partners = jnp.arange(blocks_all, dtype=jnp.int32)[:, None] + partner_offsets
    partner_data = jnp.take(spectra_blocks, partners.reshape(-1), axis=3)
    partner_data = partner_data.reshape(snaps_all, 2, bins_dev, blocks_all, PARTNERS, BLOCK)
    swapped = jnp.stack([partner_data[:, 1], -partner_data[:, 0]], axis=1)
    stacked = jnp.stack([partner_data, swapped])
    gram_tile = jnp.einsum(
        "scfbi,pscfbkj->pfbkij", spectra_blocks, stacked, preferred_element_type=jnp.float32
    )
    return (gram_tile * (1.0 / math.sqrt(snaps_all))).astype(jnp.bfloat16)


def solution(mesh):
    in_specs = (P(("fiber", "gx"), "gy"), P("fiber"), P(("fiber", "gx")), P("fiber", None))
    out_specs = P("fiber", ("gx", "gy"), None, None, None, None)

    def body(optical_phase, gauge_length, snap_starts, partner_offsets):
        ring = lax.axis_size("gx") == 8 and lax.axis_size("gy") == 2 and snap_starts.shape[0] == 2
        plan = on_device_ring if ring else on_device
        return plan(optical_phase, gauge_length, snap_starts, partner_offsets)

    return jax.shard_map(body, mesh=mesh, in_specs=in_specs, out_specs=out_specs, check_vma=False)
```

```python
import functools
import math

import jax
import jax.numpy as jnp
from jax import lax
from jax.experimental import pallas as pl
from jax.experimental.pallas import tpu as pltpu
from jax.sharding import PartitionSpec as P

BINS = 256
BLOCK = 256
SNAP_LEN = 128
GAUGE_MAX = 16
PARTNERS = 2
LANES = 128


def fourier_table(bin_index, total_len):
    sample = jnp.arange(SNAP_LEN, dtype=jnp.int32)
    product = bin_index[:, None] * sample[None, :] % total_len
    angles = 2.0 * math.pi / total_len * product.astype(jnp.float32)
    factor = 1.0 / math.sqrt(SNAP_LEN)
    return jnp.stack([jnp.cos(angles) * factor, -jnp.sin(angles) * factor]).astype(jnp.bfloat16)


def taper_window():
    sample = jnp.arange(SNAP_LEN, dtype=jnp.int32).astype(jnp.float32)
    return 0.5 - 0.5 * jnp.cos(2.0 * math.pi / SNAP_LEN * sample)


def ring_order(count):
    return [*range(0, count, 2), *range(count - 1, 0, -2)]


def shifted_table(base_ref, starts):
    return jnp.concatenate([pltpu.roll(base_ref[...], start, 1) for start in starts], axis=0).astype(jnp.bfloat16)


def stretch_spectra(out_ref, row, wide_ref, table, own, sib, gauge_ref, side):
    rows, half = own.shape
    width = 2 * half
    count = table.shape[0]
    near = pl.ds(pl.multiple_of(side * half, half), half)
    far = pl.ds(pl.multiple_of((1 - side) * half, half), half)
    wide_ref[:, near] = jnp.dot(table[:, :rows], own, preferred_element_type=jnp.float32)
    wide_ref[:, far] = jnp.dot(table[:, :rows], sib, preferred_element_type=jnp.float32)
    wide_ref[:, width : width + LANES] = jnp.broadcast_to(wide_ref[:, width - 1 : width], (count, LANES))
    span = BLOCK + LANES
    for blk in range(width // BLOCK):
        wide = wide_ref[:, blk * BLOCK : blk * BLOCK + span]
        moved = pltpu.roll(wide, span - gauge_ref[blk], 1)[:, :BLOCK]
        strain = moved - wide[:, :BLOCK]
        for tile in range(BLOCK // LANES):
            place = blk * (BLOCK // LANES) + tile
            out_ref[place, row : row + count, :] = strain[:, tile * LANES : (tile + 1) * LANES]


def starts_of(extra, half):
    values = extra.astype(jnp.float32).astype(jnp.int32)
    return values[0, 0], values[0, half // 2]


def spectra_kernel(count, rows, gauge_ref, base_ref, *refs):
    own, sib = refs[:count], refs[count : 2 * count]
    out_ref, wide_ref = refs[2 * count :]
    side = lax.axis_index("gy")
    half = own[0].shape[1]
    each = out_ref.shape[1] // count
    for n in range(count):
        table = shifted_table(base_ref, starts_of(own[n][rows:, :], half))
        stretch_spectra(
            out_ref, n * each, wide_ref.at[n % 2], table, own[n][:rows, :], sib[n][:rows, :], gauge_ref, side
        )


def spectra_group(gauge, base, rows, own, sib):
    count = len(own)
    half = own[0].shape[1]
    each = 2 * base.shape[0]
    vmem, smem = pl.BlockSpec(memory_space=pltpu.VMEM), pl.BlockSpec(memory_space=pltpu.SMEM)
    return pl.pallas_call(
        functools.partial(spectra_kernel, count, rows),
        in_specs=[smem] + [vmem] * (1 + 2 * count),
        out_specs=vmem,
        out_shape=jax.ShapeDtypeStruct((2 * half // LANES, count * each, LANES), jnp.float32),
        scratch_shapes=[pltpu.VMEM((2, each, 2 * half + LANES), jnp.float32)],
        cost_estimate=pl.CostEstimate(flops=count * 100_000_000, bytes_accessed=count * 400_000, transcendentals=0),
        name="spectra",
    )(gauge, base, *own, *sib)


def gram_kernel(
    scale, slots, unroll, gauge_ref, offset_ref, base_ref, early_ref, starts_ref,
    own0, own1, sib0, sib1, out_ref, wide_ref, spectra_ref, own_ref, sib_ref, right_ref, buf_ref, sems,
):
    side = lax.axis_index("gy")
    bins = out_ref.shape[1]
    tiles, done, _ = early_ref.shape
    width = tiles * LANES
    blocks = width // BLOCK
    cut = own0.shape[0]
    each = 2 * bins
    snaps = spectra_ref.shape[1] // each
    for whole, lower, upper in ((own_ref, own0, own1), (sib_ref, sib0, sib1)):
        whole[:cut, :] = lower[...]
        whole[cut:, :] = upper[...]
    spectra_ref[:, :done, :] = early_ref[...]
    table = shifted_table(base_ref, starts_of(starts_ref[...], width // 2))
    stretch_spectra(
        spectra_ref, done, wide_ref, table, own_ref[...], sib_ref[...], gauge_ref, side
    )

    def copies(f, slot):
        return [
            pltpu.make_async_copy(buf_ref.at[slot, part], out_ref.at[part, f], sems.at[slot, part])
            for part in range(2)
        ]

    def one(f, slot, place):
        for blk in range(blocks):
            for tile in range(BLOCK // LANES):
                at = blk * (BLOCK // LANES) + tile
                real = spectra_ref[at, pl.ds(f, snaps, stride=each), :].astype(jnp.bfloat16)
                imag = spectra_ref[at, pl.ds(bins + f, snaps, stride=each), :].astype(jnp.bfloat16)
                cols = pl.ds(tile * LANES, LANES)
                turned = pl.ds(BLOCK + tile * LANES, LANES)
                right_ref[place, blk, :snaps, cols] = real
                right_ref[place, blk, snaps:, cols] = imag
                right_ref[place, blk, :snaps, turned] = imag
                right_ref[place, blk, snaps:, turned] = -real
        for blk in range(blocks):
            for k in range(PARTNERS):
                tile = lax.dot_general(
                    right_ref[place, blk, :, :BLOCK],
                    right_ref[place, blk + offset_ref[blk, k]],
                    (((0,), (0,)), ((), ())),
                    preferred_element_type=jnp.float32,
                )
                if scale != 1.0:
                    tile = tile * scale
                buf_ref[slot, 0, blk, k] = tile[:, :BLOCK].astype(jnp.bfloat16)
                buf_ref[slot, 1, blk, k] = tile[:, BLOCK:].astype(jnp.bfloat16)
        for c in copies(f, slot):
            c.start()

    def step(i, carry):
        for u in range(unroll):
            f = i * unroll + u

            @pl.when(f >= slots)
            def _(f=f):
                for c in copies(f - slots, lax.rem(f, slots)):
                    c.wait()

        for u in range(unroll):
            f = i * unroll + u
            one(f, lax.rem(f, slots), u)
        return carry

    lax.fori_loop(0, bins // unroll, step, 0)
    for f in range(bins - slots, bins):
        for c in copies(f, f % slots):
            c.wait()


def gram(scale, gauge, offsets, base, early, starts, own, sib):
    tiles, done, _ = early.shape
    width = tiles * LANES
    bins = base.shape[0] // 2
    blocks = width // BLOCK
    rows = sum(piece.shape[0] for piece in own)
    each = 2 * base.shape[0]
    snaps = 2 * (done + each) // each
    slots, unroll = 4, 2
    vmem, smem = pl.BlockSpec(memory_space=pltpu.VMEM), pl.BlockSpec(memory_space=pltpu.SMEM)
    return pl.pallas_call(
        functools.partial(gram_kernel, scale, slots, unroll),
        in_specs=[smem] * 2 + [vmem] * 7,
        out_specs=pl.BlockSpec(memory_space=pltpu.HBM),
        out_shape=jax.ShapeDtypeStruct((2, bins, blocks, PARTNERS, BLOCK, BLOCK), jnp.bfloat16),
        scratch_shapes=[
            pltpu.VMEM((each, width + LANES), jnp.float32),
            pltpu.VMEM((tiles, done + each, LANES), jnp.float32),
            pltpu.VMEM((rows, width // 2), jnp.bfloat16),
            pltpu.VMEM((rows, width // 2), jnp.bfloat16),
            pltpu.VMEM((unroll, blocks, 2 * snaps, 2 * BLOCK), jnp.bfloat16),
            pltpu.VMEM((slots, 2, blocks, PARTNERS, BLOCK, BLOCK), jnp.bfloat16),
            pltpu.SemaphoreType.DMA((slots, 2)),
        ],
        name="gram",
    )(gauge, offsets, base, early, starts, *own, *sib)


def on_device_ring(optical_phase, gauge_length, snap_starts, partner_offsets):
    count = lax.axis_size("gx")
    pair_devices = lax.axis_size("gy")
    rows_local = optical_phase.shape[0]
    bins_dev = BINS // (count * pair_devices)
    snaps_all = count * snap_starts.shape[0]
    order = ring_order(count)
    ahead = [(order[i], order[(i + 1) % count]) for i in range(count)]
    back = [(b, a) for a, b in ahead]
    swap = [(0, 1), (1, 0)]

    scale = 1.0 / math.sqrt(snaps_all)
    root = math.sqrt(scale)
    if math.frexp(root)[0] == 0.5:
        fold, scale = root, 1.0
    else:
        fold = 1.0
    bin_index = (lax.axis_index("gx") * pair_devices + lax.axis_index("gy")) * bins_dev + jnp.arange(
        bins_dev, dtype=jnp.int32
    )

    def exchange(x):
        return lax.ppermute(x, "gy", swap)

    def tie(*xs):
        return lax.optimization_barrier(xs)

    half_rows = rows_local // 2
    half = optical_phase.shape[1]
    extra = jnp.broadcast_to(
        jnp.repeat(snap_starts, half // 2, total_repeat_length=half)[None, :], (8, half)
    ).astype(optical_phase.dtype)
    own = jnp.concatenate([optical_phase, extra], axis=0)
    f1, b1 = lax.ppermute(own, "gx", ahead), lax.ppermute(own, "gx", back)
    s_own = exchange(own)
    f1, b1 = tie(f1, b1)
    f2, b2 = lax.ppermute(f1, "gx", ahead), lax.ppermute(b1, "gx", back)
    s_f1, s_b1 = exchange(f1), exchange(b1)
    f2, b2 = tie(f2, b2)
    f3, b3 = lax.ppermute(f2, "gx", ahead), lax.ppermute(b2, "gx", back)
    s_f2, s_b2 = exchange(f2), exchange(b2)
    f3, b3 = tie(f3, b3)
    f4 = lax.ppermute(f3[:half_rows], "gx", ahead)
    b4 = lax.ppermute(b3[half_rows:], "gx", back)
    s_f3, s_b3 = exchange(f3), exchange(b3)

    fourier = fourier_table(bin_index, 2 * BINS).astype(jnp.float32) * (taper_window() * fold)
    base = fourier.astype(jnp.bfloat16).astype(jnp.float32).reshape(2 * bins_dev, SNAP_LEN)
    base = jnp.pad(base, ((0, 0), (0, SNAP_LEN)))

    early = spectra_group(
        gauge_length, base, rows_local, (own, f1, b1, f2, b2, f3, b3), (s_own, s_f1, s_b1, s_f2, s_b2, s_f3, s_b3)
    )
    f4, b4, early = tie(f4, b4, early)
    s_f4, s_b4 = exchange(f4), exchange(b4)
    own4 = (f4, b4[: rows_local - half_rows])
    sib4 = (s_f4, s_b4[: rows_local - half_rows])
    return gram(scale, gauge_length, partner_offsets, base, early, b4[rows_local - half_rows :], own4, sib4)


def strain_blocks(extended, gauges):
    blocks = gauges.shape[0]
    block_first = jnp.arange(blocks, dtype=jnp.int32) * BLOCK

    def pick_block(column):
        return lax.dynamic_slice_in_dim(extended, column, BLOCK, 1)

    shifted = jax.vmap(pick_block)(block_first + gauges)
    initial = extended[:, : blocks * BLOCK].reshape(extended.shape[0], blocks, BLOCK)
    return shifted - jnp.transpose(initial, (1, 0, 2))


def tapered_segments(strain, start_rows):
    window = taper_window()

    def segment_at(row_start):
        return lax.dynamic_slice_in_dim(strain, row_start, SNAP_LEN, 1)

    segments = jax.vmap(segment_at)(start_rows)
    return (window[None, None, :, None] * segments).astype(jnp.bfloat16)


def spectra_for(tapered, bin_index):
    fourier = fourier_table(bin_index, 2 * BINS)
    spectrum = jnp.einsum("cft,sbtj->scfbj", fourier, tapered, preferred_element_type=jnp.float32)
    shape_out = spectrum.shape
    return spectrum.astype(jnp.bfloat16).reshape(
        shape_out[0], 2, shape_out[2], shape_out[3] * BLOCK
    )


def on_device(optical_phase, gauge_length, snap_starts, partner_offsets):
    time_devices = lax.axis_size("gx")
    pair_devices = lax.axis_size("gy")
    pair_index = lax.axis_index("gy")
    rows_local = optical_phase.shape[0]
    bins_dev = BINS // (time_devices * pair_devices)
    whole_phase = lax.all_gather(optical_phase, "gy", axis=1, tiled=True)
    edge_cols = jnp.broadcast_to(whole_phase[:, -1:], (rows_local, GAUGE_MAX))
    extended = jnp.concatenate([whole_phase, edge_cols], axis=1).astype(jnp.float32)
    strain = strain_blocks(extended, gauge_length)
    tapered = tapered_segments(strain, snap_starts)
    owner_slot = jnp.arange(time_devices * bins_dev, dtype=jnp.int32)
    bin_index = (
        owner_slot // bins_dev * pair_devices + pair_index
    ) * bins_dev + owner_slot % bins_dev
    spectra = spectra_for(tapered, bin_index)
    gathered = lax.all_to_all(spectra, "gx", split_axis=2, concat_axis=0, tiled=True)
    snaps_all = gathered.shape[0]
    blocks_all = gathered.shape[3] // BLOCK
    spectra_blocks = gathered.reshape(snaps_all, 2, bins_dev, blocks_all, BLOCK)
    partners = jnp.arange(blocks_all, dtype=jnp.int32)[:, None] + partner_offsets
    partner_data = jnp.take(spectra_blocks, partners.reshape(-1), axis=3)
    partner_data = partner_data.reshape(snaps_all, 2, bins_dev, blocks_all, PARTNERS, BLOCK)
    swapped = jnp.stack([partner_data[:, 1], -partner_data[:, 0]], axis=1)
    stacked = jnp.stack([partner_data, swapped])
    gram_tile = jnp.einsum(
        "scfbi,pscfbkj->pfbkij", spectra_blocks, stacked, preferred_element_type=jnp.float32
    )
    return (gram_tile * (1.0 / math.sqrt(snaps_all))).astype(jnp.bfloat16)


def solution(mesh):
    in_specs = (P(("fiber", "gx"), "gy"), P("fiber"), P(("fiber", "gx")), P("fiber", None))
    out_specs = P("fiber", ("gx", "gy"), None, None, None, None)

    def body(optical_phase, gauge_length, snap_starts, partner_offsets):
        ring = lax.axis_size("gx") == 8 and lax.axis_size("gy") == 2 and snap_starts.shape[0] == 2
        plan = on_device_ring if ring else on_device
        return plan(optical_phase, gauge_length, snap_starts, partner_offsets)

    return jax.shard_map(body, mesh=mesh, in_specs=in_specs, out_specs=out_specs, check_vma=False)
```

```python
import functools
import math

import jax
import jax.numpy as jnp
from jax import lax
from jax.experimental import pallas as pl
from jax.experimental.pallas import tpu as pltpu
from jax.sharding import PartitionSpec as P

BINS = 256
BLOCK = 256
SNAP_LEN = 128
GAUGE_MAX = 16
PARTNERS = 2
LANES = 128


def fourier_table(bin_index, total_len):
    sample = jnp.arange(SNAP_LEN, dtype=jnp.int32)
    product = bin_index[:, None] * sample[None, :] % total_len
    angles = 2.0 * math.pi / total_len * product.astype(jnp.float32)
    factor = 1.0 / math.sqrt(SNAP_LEN)
    return jnp.stack([jnp.cos(angles) * factor, -jnp.sin(angles) * factor]).astype(jnp.bfloat16)


def taper_window():
    sample = jnp.arange(SNAP_LEN, dtype=jnp.int32).astype(jnp.float32)
    return 0.5 - 0.5 * jnp.cos(2.0 * math.pi / SNAP_LEN * sample)


def ring_order(count):
    return [*range(0, count, 2), *range(count - 1, 0, -2)]


def ring_device(step, count):
    me = lax.axis_index("gx")
    place = jnp.where(me % 2 == 0, me // 2, count // 2 + (count - 1 - me) // 2)
    at = (place + step + count) % count
    return jnp.where(at < count // 2, 2 * at, count - 1 - 2 * (at - count // 2))


def starts_of(starts_ref, step, count, snaps):
    slot = lax.axis_index("gx") ^ ring_device(step, count)
    return [starts_ref[slot * snaps + n] for n in range(snaps)]


def shifted_table(base, starts):
    return jnp.concatenate([pltpu.roll(base, start, 1) for start in starts], axis=0).astype(jnp.bfloat16)


def spectra_kernel(steps, count, snaps, starts_ref, base_ref, *refs):
    stretches = refs[: len(steps)]
    near_ref, far_ref, held_ref, sems = refs[len(steps) :]
    copies = [
        pltpu.make_async_copy(ref, held_ref.at[n], sems.at[n]) for n, ref in enumerate(stretches)
    ]
    for c in copies:
        c.start()
    rows = held_ref.shape[1]
    tiles = near_ref.shape[0]
    each = base_ref.shape[0] // 2
    for n, step in enumerate(steps):
        table = shifted_table(base_ref[...], starts_of(starts_ref, step, count, snaps))[:, :rows]
        copies[n].wait()
        out = jnp.dot(table, held_ref[n], preferred_element_type=jnp.float32)
        for snap in range(snaps):
            for part, ref in enumerate((near_ref, far_ref)):
                at = (snap * 2 + part) * each
                to = (n * snaps + snap) * each
                for tile in range(tiles):
                    ref[tile, to : to + each, :] = out[at : at + each, tile * LANES : (tile + 1) * LANES]


def spectra_group(steps, count, snaps, starts, base, stretches):
    rows, half = stretches[0].shape
    each = base.shape[0] // 2
    shape = jax.ShapeDtypeStruct((half // LANES, len(steps) * snaps * each, LANES), jnp.float32)
    vmem, smem = pl.BlockSpec(memory_space=pltpu.VMEM), pl.BlockSpec(memory_space=pltpu.SMEM)
    return pl.pallas_call(
        functools.partial(spectra_kernel, steps, count, snaps),
        in_specs=[smem, vmem] + [pl.BlockSpec(memory_space=pl.ANY)] * len(steps),
        out_specs=(vmem, vmem),
        out_shape=(shape, shape),
        scratch_shapes=[
            pltpu.VMEM((len(steps), rows, half), jnp.bfloat16),
            pltpu.SemaphoreType.DMA((len(steps),)),
        ],
        cost_estimate=pl.CostEstimate(
            flops=len(steps) * 100_000_000, bytes_accessed=len(steps) * 400_000, transcendentals=0
        ),
        compiler_params=pltpu.CompilerParams(vmem_limit_bytes=8 << 20),
        name="spectra",
    )(starts, base, *stretches)


def gram_kernel(
    groups, count, snaps, scale, slots, unroll, gauge_ref, starts_ref, offset_ref, base_ref, *refs
):
    early = refs[: 2 * groups]
    last = refs[2 * groups : 2 * groups + 4]
    out_ref, spectra_ref, last_ref, right_ref, buf_ref, early_sems, last_sems, sems = refs[2 * groups + 4 :]
    side = lax.axis_index("gy")
    bins = out_ref.shape[1]
    tiles, total, _ = spectra_ref.shape
    half = tiles // 2
    blocks = tiles * LANES // BLOCK
    each = 2 * bins
    cut = last[0].shape[0]
    rows = last_ref.shape[1]
    cores = (pl.ds(side * half, half), pl.ds((1 - side) * half, half))

    waits, done = [], 0
    for n, ref in enumerate(early):
        at = pl.ds(done, ref.shape[1])
        waits.append(pltpu.make_async_copy(ref, spectra_ref.at[cores[n % 2], at], early_sems.at[n]))
        done += ref.shape[1] * (n % 2)
    for n, ref in enumerate(last):
        at = pl.ds(0, cut) if n % 2 == 0 else pl.ds(cut, rows - cut)
        waits.append(pltpu.make_async_copy(ref, last_ref.at[n // 2, at], last_sems.at[n]))
    for c in waits:
        c.start()
    table = shifted_table(base_ref[:each, :], starts_of(starts_ref, count // 2, count, snaps))[:, :rows]
    for c in waits[2 * groups :]:
        c.wait()
    for core in range(2):
        out = jnp.dot(table, last_ref[core], preferred_element_type=jnp.float32)
        for tile in range(half):
            place = side * half + tile if core == 0 else (1 - side) * half + tile
            spectra_ref[place, done:, :] = out[:, tile * LANES : (tile + 1) * LANES]
    for c in waits[: 2 * groups]:
        c.wait()

    def copies(f, slot):
        return [
            pltpu.make_async_copy(buf_ref.at[slot, part], out_ref.at[part, f], sems.at[slot, part])
            for part in range(2)
        ]

    def strain_spectra(row):
        held = [spectra_ref[tile, pl.ds(row, total // each, stride=each), :] for tile in range(tiles)]
        held.append(jnp.broadcast_to(held[-1][:, LANES - 1 :], held[-1].shape))
        per_block = BLOCK // LANES
        span = BLOCK + LANES
        for blk in range(blocks):
            wide = jnp.concatenate(held[blk * per_block : (blk + 1) * per_block + 1], axis=1)
            moved = pltpu.roll(wide, span - gauge_ref[blk], 1)[:, :BLOCK]
            yield (moved - wide[:, :BLOCK]).astype(jnp.bfloat16)

    def one(f, slot, place):
        many = total // each
        for blk, (real, imag) in enumerate(zip(strain_spectra(f), strain_spectra(bins + f), strict=True)):
            right_ref[place, blk, :many, :BLOCK] = real
            right_ref[place, blk, many:, :BLOCK] = imag
            right_ref[place, blk, :many, BLOCK:] = imag
            right_ref[place, blk, many:, BLOCK:] = -real
        for blk in range(blocks):
            for k in range(PARTNERS):
                tile = lax.dot_general(
                    right_ref[place, blk, :, :BLOCK],
                    right_ref[place, blk + offset_ref[k, blk]],
                    (((0,), (0,)), ((), ())),
                    preferred_element_type=jnp.float32,
                )
                if scale != 1.0:
                    tile = tile * scale
                buf_ref[slot, 0, blk, k] = tile[:, :BLOCK].astype(jnp.bfloat16)
                buf_ref[slot, 1, blk, k] = tile[:, BLOCK:].astype(jnp.bfloat16)
        for c in copies(f, slot):
            c.start()

    def step(i, carry):
        for u in range(unroll):
            f = i * unroll + u

            @pl.when(f >= slots)
            def _(f=f):
                for c in copies(f - slots, lax.rem(f, slots)):
                    c.wait()

        for u in range(unroll):
            f = i * unroll + u
            one(f, lax.rem(f, slots), u)
        return carry

    lax.fori_loop(0, bins // unroll, step, 0)
    for f in range(bins - slots, bins):
        for c in copies(f, f % slots):
            c.wait()


def gram(count, snaps, scale, gauge, starts, offsets, base, early, own, sib):
    half = early[0].shape[0]
    bins = base.shape[0] // 4
    blocks = 2 * half * LANES // BLOCK
    rows = sum(piece.shape[0] for piece in own)
    total = count * snaps * 2 * bins
    slots, unroll = 4, 2
    vmem, smem = pl.BlockSpec(memory_space=pltpu.VMEM), pl.BlockSpec(memory_space=pltpu.SMEM)
    return pl.pallas_call(
        functools.partial(gram_kernel, len(early) // 2, count, snaps, scale, slots, unroll),
        in_specs=[smem] * 3 + [vmem] + [pl.BlockSpec(memory_space=pl.ANY)] * (len(early) + 4),
        out_specs=pl.BlockSpec(memory_space=pltpu.HBM),
        out_shape=jax.ShapeDtypeStruct((2, bins, blocks, PARTNERS, BLOCK, BLOCK), jnp.bfloat16),
        scratch_shapes=[
            pltpu.VMEM((2 * half, total, LANES), jnp.float32),
            pltpu.VMEM((2, rows, half * LANES), jnp.bfloat16),
            pltpu.VMEM((unroll, blocks, 2 * count * snaps, 2 * BLOCK), jnp.bfloat16),
            pltpu.VMEM((slots, 2, blocks, PARTNERS, BLOCK, BLOCK), jnp.bfloat16),
            pltpu.SemaphoreType.DMA((len(early),)),
            pltpu.SemaphoreType.DMA((4,)),
            pltpu.SemaphoreType.DMA((slots, 2)),
        ],
        compiler_params=pltpu.CompilerParams(vmem_limit_bytes=24 << 20),
        name="gram",
    )(gauge, starts, offsets, base, *early, *own, *sib)


def on_device_ring(optical_phase, gauge_length, snap_starts, partner_offsets):
    count = lax.axis_size("gx")
    pair_devices = lax.axis_size("gy")
    rows_local = optical_phase.shape[0]
    bins_dev = BINS // (count * pair_devices)
    snaps = snap_starts.shape[0]
    order = ring_order(count)
    ahead = [(order[i], order[(i + 1) % count]) for i in range(count)]
    back = [(b, a) for a, b in ahead]

    scale = 1.0 / math.sqrt(count * snaps)
    root = math.sqrt(scale)
    if math.frexp(root)[0] == 0.5:
        fold, scale = root, 1.0
    else:
        fold = 1.0

    cores = lax.axis_index("gy") ^ jnp.arange(pair_devices, dtype=jnp.int32)
    first_bin = (lax.axis_index("gx") * pair_devices + cores) * bins_dev
    bin_index = (first_bin[:, None] + jnp.arange(bins_dev, dtype=jnp.int32)[None, :]).reshape(-1)
    fourier = fourier_table(bin_index, 2 * BINS).astype(jnp.float32) * (taper_window() * fold)
    base = fourier.astype(jnp.bfloat16).astype(jnp.float32).reshape(2, pair_devices, bins_dev, SNAP_LEN)
    base = jnp.transpose(base, (1, 0, 2, 3)).reshape(2 * pair_devices * bins_dev, SNAP_LEN)
    base = jnp.pad(base, ((0, 0), (0, SNAP_LEN)))

    def exchange(x):
        return lax.ppermute(x, "gy", [(0, 1), (1, 0)])

    def tie(*xs):
        return lax.optimization_barrier(xs)

    def spectra(steps, *stretches):
        return spectra_group(steps, count, snaps, starts, base, stretches)

    def with_other(x, bit):
        return jnp.concatenate([x, lax.ppermute(x, "gx", [(i, i ^ bit) for i in range(count)])])

    half_rows = rows_local // 2
    own = optical_phase
    f1, b1 = lax.ppermute(own, "gx", ahead), lax.ppermute(own, "gx", back)
    starts = with_other(snap_starts, 1)
    f1, b1, starts = tie(f1, b1, starts)
    f2, b2 = lax.ppermute(f1, "gx", ahead), lax.ppermute(b1, "gx", back)
    starts = with_other(starts, 2)
    starts = with_other(starts, 4)
    f2, b2, starts, base = tie(f2, b2, starts, base)
    f3, b3 = lax.ppermute(f2, "gx", ahead), lax.ppermute(b2, "gx", back)
    near1, far1 = spectra((0, -1, 1, -2, 2), own, f1, b1, f2, b2)
    f3, b3, near1, far1 = tie(f3, b3, near1, far1)
    f4 = lax.ppermute(f3[:half_rows], "gx", ahead)
    b4 = lax.ppermute(b3[half_rows:], "gx", back)
    other1 = exchange(far1)
    near2, far2 = spectra((-3, 3), f3, b3)
    f4, b4, near2, far2 = tie(f4, b4, near2, far2)
    other2 = exchange(far2)
    own4, sib4 = (f4, b4), (exchange(f4), exchange(b4))
    return gram(
        count, snaps, scale, gauge_length, starts, partner_offsets.T, base, (near1, other1, near2, other2), own4, sib4
    )


def strain_blocks(extended, gauges):
    blocks = gauges.shape[0]
    block_first = jnp.arange(blocks, dtype=jnp.int32) * BLOCK

    def pick_block(column):
        return lax.dynamic_slice_in_dim(extended, column, BLOCK, 1)

    shifted = jax.vmap(pick_block)(block_first + gauges)
    initial = extended[:, : blocks * BLOCK].reshape(extended.shape[0], blocks, BLOCK)
    return shifted - jnp.transpose(initial, (1, 0, 2))


def tapered_segments(strain, start_rows):
    window = taper_window()

    def segment_at(row_start):
        return lax.dynamic_slice_in_dim(strain, row_start, SNAP_LEN, 1)

    segments = jax.vmap(segment_at)(start_rows)
    return (window[None, None, :, None] * segments).astype(jnp.bfloat16)


def spectra_for(tapered, bin_index):
    fourier = fourier_table(bin_index, 2 * BINS)
    spectrum = jnp.einsum("cft,sbtj->scfbj", fourier, tapered, preferred_element_type=jnp.float32)
    shape_out = spectrum.shape
    return spectrum.astype(jnp.bfloat16).reshape(
        shape_out[0], 2, shape_out[2], shape_out[3] * BLOCK
    )


def on_device(optical_phase, gauge_length, snap_starts, partner_offsets):
    time_devices = lax.axis_size("gx")
    pair_devices = lax.axis_size("gy")
    pair_index = lax.axis_index("gy")
    rows_local = optical_phase.shape[0]
    bins_dev = BINS // (time_devices * pair_devices)
    whole_phase = lax.all_gather(optical_phase, "gy", axis=1, tiled=True)
    edge_cols = jnp.broadcast_to(whole_phase[:, -1:], (rows_local, GAUGE_MAX))
    extended = jnp.concatenate([whole_phase, edge_cols], axis=1).astype(jnp.float32)
    strain = strain_blocks(extended, gauge_length)
    tapered = tapered_segments(strain, snap_starts)
    owner_slot = jnp.arange(time_devices * bins_dev, dtype=jnp.int32)
    bin_index = (
        owner_slot // bins_dev * pair_devices + pair_index
    ) * bins_dev + owner_slot % bins_dev
    spectra = spectra_for(tapered, bin_index)
    gathered = lax.all_to_all(spectra, "gx", split_axis=2, concat_axis=0, tiled=True)
    snaps_all = gathered.shape[0]
    blocks_all = gathered.shape[3] // BLOCK
    spectra_blocks = gathered.reshape(snaps_all, 2, bins_dev, blocks_all, BLOCK)
    partners = jnp.arange(blocks_all, dtype=jnp.int32)[:, None] + partner_offsets
    partner_data = jnp.take(spectra_blocks, partners.reshape(-1), axis=3)
    partner_data = partner_data.reshape(snaps_all, 2, bins_dev, blocks_all, PARTNERS, BLOCK)
    swapped = jnp.stack([partner_data[:, 1], -partner_data[:, 0]], axis=1)
    stacked = jnp.stack([partner_data, swapped])
    gram_tile = jnp.einsum(
        "scfbi,pscfbkj->pfbkij", spectra_blocks, stacked, preferred_element_type=jnp.float32
    )
    return (gram_tile * (1.0 / math.sqrt(snaps_all))).astype(jnp.bfloat16)


def solution(mesh):
    in_specs = (P(("fiber", "gx"), "gy"), P("fiber"), P(("fiber", "gx")), P("fiber", None))
    out_specs = P("fiber", ("gx", "gy"), None, None, None, None)

    def body(optical_phase, gauge_length, snap_starts, partner_offsets):
        ring = lax.axis_size("gx") == 8 and lax.axis_size("gy") == 2 and snap_starts.shape[0] == 2
        plan = on_device_ring if ring else on_device
        return plan(optical_phase, gauge_length, snap_starts, partner_offsets)

    return jax.shard_map(body, mesh=mesh, in_specs=in_specs, out_specs=out_specs, check_vma=False)
```

```python
import functools
import math

import jax
import jax.numpy as jnp
from jax import lax
from jax.experimental import pallas as pl
from jax.experimental.pallas import tpu as pltpu
from jax.sharding import PartitionSpec as P


BINS = 256
BLOCK = 256
SNAP_LEN = 128
GAUGE_MAX = 16
PARTNERS = 2
LANES = 128


def fourier_table(bin_index, total_len):
    sample = jnp.arange(SNAP_LEN, dtype=jnp.int32)
    product = bin_index[:, None] * sample[None, :] % total_len
    angles = 2.0 * math.pi / total_len * product.astype(jnp.float32)
    factor = 1.0 / math.sqrt(SNAP_LEN)
    return jnp.stack([jnp.cos(angles) * factor, -jnp.sin(angles) * factor]).astype(jnp.bfloat16)


def taper_window():
    sample = jnp.arange(SNAP_LEN, dtype=jnp.int32).astype(jnp.float32)
    return 0.5 - 0.5 * jnp.cos(2.0 * math.pi / SNAP_LEN * sample)


def ring_order(count):
    return [*range(0, count, 2), *range(count - 1, 0, -2)]


def starts_in(extra, snaps):
    values = extra.astype(jnp.float32).astype(jnp.int32)
    return [values[n * (8 // snaps), 0] for n in range(snaps)]


def shifted_table(base, starts):
    return jnp.concatenate([pltpu.roll(base, start, 1) for start in starts], axis=0).astype(jnp.bfloat16)


def spectra_kernel(snaps, base_ref, *refs):
    near_ref, far_ref, held_ref, sems = refs[-4:]
    stretches = refs[:-4]
    copies = [
        pltpu.make_async_copy(ref, held_ref.at[n], sems.at[n]) for n, ref in enumerate(stretches)
    ]
    for c in copies:
        c.start()
    rows = held_ref.shape[1] - 8
    tiles = near_ref.shape[0]
    each = base_ref.shape[0] // 2
    for n in range(len(stretches)):
        copies[n].wait()
        table = shifted_table(base_ref[...], starts_in(held_ref[n, rows:, :], snaps))[:, :rows]
        out = jnp.dot(table, held_ref[n, :rows, :], preferred_element_type=jnp.float32)
        for snap in range(snaps):
            for part, ref in enumerate((near_ref, far_ref)):
                at = (snap * 2 + part) * each
                to = (n * snaps + snap) * each
                for tile in range(tiles):
                    ref[tile, to : to + each, :] = out[at : at + each, tile * LANES : (tile + 1) * LANES]


def spectra_group(snaps, base, stretches):
    rows, half = stretches[0].shape
    each = base.shape[0] // 2
    count = len(stretches)
    shape = jax.ShapeDtypeStruct((half // LANES, count * snaps * each, LANES), jnp.float32)
    vmem = pl.BlockSpec(memory_space=pltpu.VMEM)
    return pl.pallas_call(
        functools.partial(spectra_kernel, snaps),
        in_specs=[vmem] + [pl.BlockSpec(memory_space=pl.ANY)] * count,
        out_specs=(vmem, vmem),
        out_shape=(shape, shape),
        scratch_shapes=[
            pltpu.VMEM((count, rows, half), jnp.bfloat16),
            pltpu.SemaphoreType.DMA((count,)),
        ],
        cost_estimate=pl.CostEstimate(
            flops=count * 100_000_000, bytes_accessed=count * 400_000, transcendentals=0
        ),
        compiler_params=pltpu.CompilerParams(vmem_limit_bytes=8 << 20),
        name="spectra",
    )(base, *stretches)


def gram_kernel(
    groups, snaps, scale, slots, unroll, meta_ref, base_ref, *refs
):
    early = refs[: 2 * groups]
    last = refs[2 * groups : 2 * groups + 4]
    out_ref, spectra_ref, last_ref, extra_ref, right_ref, buf_ref, early_sems, last_sems, sems = refs[2 * groups + 4 :]
    side = lax.axis_index("gy")
    bins = out_ref.shape[1]
    tiles, total, _ = spectra_ref.shape
    half = tiles // 2
    blocks = tiles * LANES // BLOCK
    each = 2 * bins
    cut = last[0].shape[0]
    rows = last_ref.shape[1]
    cores = (pl.ds(side * half, half), pl.ds((1 - side) * half, half))

    waits, done = [], 0
    for n, ref in enumerate(early):
        at = pl.ds(done, ref.shape[1])
        waits.append(pltpu.make_async_copy(ref, spectra_ref.at[cores[n % 2], at], early_sems.at[n]))
        done += ref.shape[1] * (n % 2)
    for n, ref in enumerate(last):
        at = pl.ds(0, cut) if n % 2 == 0 else pl.ds(cut, rows - cut)
        piece = ref if n % 2 == 0 else ref.at[pl.ds(0, rows - cut)]
        waits.append(pltpu.make_async_copy(piece, last_ref.at[n // 2, at], last_sems.at[n]))
    waits.append(pltpu.make_async_copy(last[1].at[pl.ds(rows - cut, 8)], extra_ref, last_sems.at[4]))
    for c in waits:
        c.start()
    waits[-1].wait()
    table = shifted_table(base_ref[:each, :], starts_in(extra_ref[...], snaps))[:, :rows]
    for c in waits[2 * groups : -1]:
        c.wait()
    for core in range(2):
        out = jnp.dot(table, last_ref[core], preferred_element_type=jnp.float32)
        for tile in range(half):
            place = side * half + tile if core == 0 else (1 - side) * half + tile
            spectra_ref[place, done:, :] = out[:, tile * LANES : (tile + 1) * LANES]
    for c in waits[: 2 * groups]:
        c.wait()

    def copies(f, slot):
        return [
            pltpu.make_async_copy(buf_ref.at[slot, part], out_ref.at[part, f], sems.at[slot, part])
            for part in range(2)
        ]

    def strain_spectra(row):
        held = [spectra_ref[tile, pl.ds(row, total // each, stride=each), :] for tile in range(tiles)]
        held.append(jnp.broadcast_to(held[-1][:, LANES - 1 :], held[-1].shape))
        per_block = BLOCK // LANES
        span = BLOCK + LANES
        for blk in range(blocks):
            wide = jnp.concatenate(held[blk * per_block : (blk + 1) * per_block + 1], axis=1)
            moved = pltpu.roll(wide, span - meta_ref[blk], 1)[:, :BLOCK]
            yield (moved - wide[:, :BLOCK]).astype(jnp.bfloat16)

    def one(f, slot, place):
        many = total // each
        for blk, (real, imag) in enumerate(zip(strain_spectra(f), strain_spectra(bins + f), strict=True)):
            right_ref[place, blk, :many, :BLOCK] = real
            right_ref[place, blk, many:, :BLOCK] = imag
            right_ref[place, blk, :many, BLOCK:] = imag
            right_ref[place, blk, many:, BLOCK:] = -real
        for blk in range(blocks):
            for k in range(PARTNERS):
                tile = lax.dot_general(
                    right_ref[place, blk, :, :BLOCK],
                    right_ref[place, blk + meta_ref[blocks * (1 + k) + blk]],
                    (((0,), (0,)), ((), ())),
                    preferred_element_type=jnp.float32,
                )
                if scale != 1.0:
                    tile = tile * scale
                buf_ref[slot, 0, blk, k] = tile[:, :BLOCK].astype(jnp.bfloat16)
                buf_ref[slot, 1, blk, k] = tile[:, BLOCK:].astype(jnp.bfloat16)
        for c in copies(f, slot):
            c.start()

    def step(i, carry):
        for u in range(unroll):
            f = i * unroll + u

            @pl.when(f >= slots)
            def _(f=f):
                for c in copies(f - slots, lax.rem(f, slots)):
                    c.wait()

        for u in range(unroll):
            f = i * unroll + u
            one(f, lax.rem(f, slots), u)
        return carry

    lax.fori_loop(0, bins // unroll, step, 0)
    for f in range(bins - slots, bins):
        for c in copies(f, f % slots):
            c.wait()


def gram(count, snaps, scale, meta, base, early, own, sib):
    half = early[0].shape[0]
    bins = base.shape[0] // 4
    blocks = 2 * half * LANES // BLOCK
    rows = sum(piece.shape[0] for piece in own) - 8
    total = count * snaps * 2 * bins
    slots, unroll = 4, 2
    vmem, smem = pl.BlockSpec(memory_space=pltpu.VMEM), pl.BlockSpec(memory_space=pltpu.SMEM)
    return pl.pallas_call(
        functools.partial(gram_kernel, len(early) // 2, snaps, scale, slots, unroll),
        in_specs=[smem, vmem] + [pl.BlockSpec(memory_space=pl.ANY)] * (len(early) + 4),
        out_specs=pl.BlockSpec(memory_space=pltpu.HBM),
        out_shape=jax.ShapeDtypeStruct((2, bins, blocks, PARTNERS, BLOCK, BLOCK), jnp.bfloat16),
        scratch_shapes=[
            pltpu.VMEM((2 * half, total, LANES), jnp.float32),
            pltpu.VMEM((2, rows, half * LANES), jnp.bfloat16),
            pltpu.VMEM((8, half * LANES), jnp.bfloat16),
            pltpu.VMEM((unroll, blocks, 2 * count * snaps, 2 * BLOCK), jnp.bfloat16),
            pltpu.VMEM((slots, 2, blocks, PARTNERS, BLOCK, BLOCK), jnp.bfloat16),
            pltpu.SemaphoreType.DMA((len(early),)),
            pltpu.SemaphoreType.DMA((5,)),
            pltpu.SemaphoreType.DMA((slots, 2)),
        ],
        compiler_params=pltpu.CompilerParams(vmem_limit_bytes=24 << 20),
        name="gram",
    )(meta, base, *early, *own, *sib)


def on_device_ring(optical_phase, gauge_length, snap_starts, partner_offsets):
    count = lax.axis_size("gx")
    pair_devices = lax.axis_size("gy")
    rows_local = optical_phase.shape[0]
    bins_dev = BINS // (count * pair_devices)
    snaps = snap_starts.shape[0]
    order = ring_order(count)
    ahead = [(order[i], order[(i + 1) % count]) for i in range(count)]
    back = [(b, a) for a, b in ahead]

    scale = 1.0 / math.sqrt(count * snaps)
    root = math.sqrt(scale)
    if math.frexp(root)[0] == 0.5:
        fold, scale = root, 1.0
    else:
        fold = 1.0

    cores = lax.axis_index("gy") ^ jnp.arange(pair_devices, dtype=jnp.int32)
    first_bin = (lax.axis_index("gx") * pair_devices + cores) * bins_dev
    bin_index = (first_bin[:, None] + jnp.arange(bins_dev, dtype=jnp.int32)[None, :]).reshape(-1)
    fourier = fourier_table(bin_index, 2 * BINS).astype(jnp.float32) * (taper_window() * fold)
    base = fourier.astype(jnp.bfloat16).astype(jnp.float32).reshape(2, pair_devices, bins_dev, SNAP_LEN)
    base = jnp.transpose(base, (1, 0, 2, 3)).reshape(2 * pair_devices * bins_dev, SNAP_LEN)
    base = jnp.pad(base, ((0, 0), (0, SNAP_LEN)))

    def exchange(x):
        return lax.ppermute(x, "gy", [(0, 1), (1, 0)])

    def tie(*xs):
        return lax.optimization_barrier(xs)

    def spectra(*stretches):
        return spectra_group(snaps, base, stretches)

    def onward(f, b):
        return lax.ppermute(f, "gx", ahead), lax.ppermute(b, "gx", back)

    half_rows = rows_local // 2
    half = optical_phase.shape[1]
    extra = snap_starts.astype(optical_phase.dtype)[:, None, None]
    extra = jnp.broadcast_to(extra, (snaps, 8 // snaps, half)).reshape(8, half)
    f1, b1 = onward(optical_phase, optical_phase)
    ef, eb = lax.ppermute(extra, "gx", ahead), lax.ppermute(extra, "gx", back)
    f1, b1 = jnp.concatenate([f1, ef]), jnp.concatenate([b1, eb])
    own = jnp.concatenate([optical_phase, extra])
    meta = jnp.concatenate([gauge_length, partner_offsets.T.reshape(-1)])
    f1, b1, own, base, meta = tie(f1, b1, own, base, meta)
    f2, b2 = onward(f1, b1)
    near1, far1 = spectra(own, f1, b1)
    f2, b2, near1, far1 = tie(f2, b2, near1, far1)
    f3, b3 = onward(f2, b2)
    other1 = exchange(far1)
    near2, far2 = spectra(f2, b2)
    f3, b3, near2, far2 = tie(f3, b3, near2, far2)
    f4, b4 = onward(f3[:half_rows], b3[half_rows:])
    other2 = exchange(far2)
    near3, far3 = spectra(f3, b3)
    f4, b4, near3, far3 = tie(f4, b4, near3, far3)
    own4, sib4 = (f4, b4), (exchange(f4), exchange(b4))
    other3 = exchange(far3)
    early = (near1, other1, near2, other2, near3, other3)
    return gram(count, snaps, scale, meta, base, early, own4, sib4)


def strain_blocks(extended, gauges):
    blocks = gauges.shape[0]
    block_first = jnp.arange(blocks, dtype=jnp.int32) * BLOCK

    def pick_block(column):
        return lax.dynamic_slice_in_dim(extended, column, BLOCK, 1)

    shifted = jax.vmap(pick_block)(block_first + gauges)
    initial = extended[:, : blocks * BLOCK].reshape(extended.shape[0], blocks, BLOCK)
    return shifted - jnp.transpose(initial, (1, 0, 2))


def tapered_segments(strain, start_rows):
    window = taper_window()

    def segment_at(row_start):
        return lax.dynamic_slice_in_dim(strain, row_start, SNAP_LEN, 1)

    segments = jax.vmap(segment_at)(start_rows)
    return (window[None, None, :, None] * segments).astype(jnp.bfloat16)


def spectra_for(tapered, bin_index):
    fourier = fourier_table(bin_index, 2 * BINS)
    spectrum = jnp.einsum("cft,sbtj->scfbj", fourier, tapered, preferred_element_type=jnp.float32)
    shape_out = spectrum.shape
    return spectrum.astype(jnp.bfloat16).reshape(
        shape_out[0], 2, shape_out[2], shape_out[3] * BLOCK
    )


def on_device(optical_phase, gauge_length, snap_starts, partner_offsets):
    time_devices = lax.axis_size("gx")
    pair_devices = lax.axis_size("gy")
    pair_index = lax.axis_index("gy")
    rows_local = optical_phase.shape[0]
    bins_dev = BINS // (time_devices * pair_devices)
    whole_phase = lax.all_gather(optical_phase, "gy", axis=1, tiled=True)
    edge_cols = jnp.broadcast_to(whole_phase[:, -1:], (rows_local, GAUGE_MAX))
    extended = jnp.concatenate([whole_phase, edge_cols], axis=1).astype(jnp.float32)
    strain = strain_blocks(extended, gauge_length)
    tapered = tapered_segments(strain, snap_starts)
    owner_slot = jnp.arange(time_devices * bins_dev, dtype=jnp.int32)
    bin_index = (
        owner_slot // bins_dev * pair_devices + pair_index
    ) * bins_dev + owner_slot % bins_dev
    spectra = spectra_for(tapered, bin_index)
    gathered = lax.all_to_all(spectra, "gx", split_axis=2, concat_axis=0, tiled=True)
    snaps_all = gathered.shape[0]
    blocks_all = gathered.shape[3] // BLOCK
    spectra_blocks = gathered.reshape(snaps_all, 2, bins_dev, blocks_all, BLOCK)
    partners = jnp.arange(blocks_all, dtype=jnp.int32)[:, None] + partner_offsets
    partner_data = jnp.take(spectra_blocks, partners.reshape(-1), axis=3)
    partner_data = partner_data.reshape(snaps_all, 2, bins_dev, blocks_all, PARTNERS, BLOCK)
    swapped = jnp.stack([partner_data[:, 1], -partner_data[:, 0]], axis=1)
    stacked = jnp.stack([partner_data, swapped])
    gram_tile = jnp.einsum(
        "scfbi,pscfbkj->pfbkij", spectra_blocks, stacked, preferred_element_type=jnp.float32
    )
    return (gram_tile * (1.0 / math.sqrt(snaps_all))).astype(jnp.bfloat16)


def solution(mesh):
    in_specs = (P(("fiber", "gx"), "gy"), P("fiber"), P(("fiber", "gx")), P("fiber", None))
    out_specs = P("fiber", ("gx", "gy"), None, None, None, None)

    def body(optical_phase, gauge_length, snap_starts, partner_offsets):
        ring = lax.axis_size("gx") == 8 and lax.axis_size("gy") == 2 and snap_starts.shape[0] == 2
        plan = on_device_ring if ring else on_device
        return plan(optical_phase, gauge_length, snap_starts, partner_offsets)

    return jax.shard_map(body, mesh=mesh, in_specs=in_specs, out_specs=out_specs, check_vma=False)
```

```python
import functools
import math

import jax
import jax.numpy as jnp
from jax import lax
from jax.experimental import pallas as pl
from jax.experimental.pallas import tpu as pltpu
from jax.sharding import PartitionSpec as P


BINS = 256
BLOCK = 256
SNAP_LEN = 128
GAUGE_MAX = 16
PARTNERS = 2
LANES = 128


def fourier_table(bin_index, total_len):
    sample = jnp.arange(SNAP_LEN, dtype=jnp.int32)
    product = bin_index[:, None] * sample[None, :] % total_len
    angles = 2.0 * math.pi / total_len * product.astype(jnp.float32)
    factor = 1.0 / math.sqrt(SNAP_LEN)
    return jnp.stack([jnp.cos(angles) * factor, -jnp.sin(angles) * factor]).astype(jnp.bfloat16)


def taper_window():
    sample = jnp.arange(SNAP_LEN, dtype=jnp.int32).astype(jnp.float32)
    return 0.5 - 0.5 * jnp.cos(2.0 * math.pi / SNAP_LEN * sample)


def ring_order(count):
    return [*range(0, count, 2), *range(count - 1, 0, -2)]


def starts_in(extra, snaps):
    values = extra.astype(jnp.float32).astype(jnp.int32)
    return [values[n * (8 // snaps), 0] for n in range(snaps)]


def shifted_table(base, starts):
    return jnp.concatenate([pltpu.roll(base, start, 1) for start in starts], axis=0).astype(jnp.bfloat16)


def spectra_kernel(snaps, base_ref, *refs):
    *stretches, near_ref, far_ref = refs
    rows = stretches[0].shape[0] - 8
    tiles = near_ref.shape[0]
    each = base_ref.shape[0] // 2
    for n, ref in enumerate(stretches):
        table = shifted_table(base_ref[...], starts_in(ref[rows:, :], snaps))[:, :rows]
        out = jnp.dot(table, ref[:rows, :], preferred_element_type=jnp.float32)
        for snap in range(snaps):
            for part, to_ref in enumerate((near_ref, far_ref)):
                at = (snap * 2 + part) * each
                to = (n * snaps + snap) * each
                for tile in range(tiles):
                    to_ref[tile, to : to + each, :] = out[at : at + each, tile * LANES : (tile + 1) * LANES]


def spectra_group(snaps, base, stretches):
    half = stretches[0].shape[1]
    each = base.shape[0] // 2
    count = len(stretches)
    shape = jax.ShapeDtypeStruct((half // LANES, count * snaps * each, LANES), jnp.float32)
    vmem = pl.BlockSpec(memory_space=pltpu.VMEM)
    return pl.pallas_call(
        functools.partial(spectra_kernel, snaps),
        in_specs=[vmem] * (1 + count),
        out_specs=(vmem, vmem),
        out_shape=(shape, shape),
        cost_estimate=pl.CostEstimate(
            flops=count * 100_000_000, bytes_accessed=count * 400_000, transcendentals=0
        ),
        compiler_params=pltpu.CompilerParams(vmem_limit_bytes=8 << 20),
        name="spectra",
    )(base, *stretches)


def gram_kernel(groups, snaps, scale, slots, meta_ref, base_ref, *refs):
    early = refs[: 2 * groups]
    own0, own1, sib0, sib1 = refs[2 * groups : 2 * groups + 4]
    out_ref, spectra_ref, even_ref, odd_ref, buf_ref, sems = refs[2 * groups + 4 :]
    side = lax.axis_index("gy")
    bins = out_ref.shape[1]
    tiles, total, _ = spectra_ref.shape
    half = tiles // 2
    blocks = tiles * LANES // BLOCK
    each = 2 * bins
    many = total // each
    rows = own0.shape[0] + own1.shape[0] - 8
    cut = own0.shape[0]

    done = 0
    for n, ref in enumerate(early):
        side_of = side if n % 2 == 0 else 1 - side
        for tile in range(half):
            spectra_ref[side_of * half + tile, done : done + ref.shape[1], :] = ref[tile]
        done += ref.shape[1] * (n % 2)
    table = shifted_table(base_ref[:each, :], starts_in(own1[rows - cut :, :], snaps))[:, :rows]
    for core, (lower, upper) in enumerate(((own0, own1), (sib0, sib1))):
        phase = jnp.concatenate([lower[...], upper[: rows - cut, :]], axis=0)
        out = jnp.dot(table, phase, preferred_element_type=jnp.float32)
        side_of = side if core == 0 else 1 - side
        for tile in range(half):
            spectra_ref[side_of * half + tile, done:, :] = out[:, tile * LANES : (tile + 1) * LANES]

    def copies(f, slot):
        return [
            pltpu.make_async_copy(buf_ref.at[slot, part], out_ref.at[part, f], sems.at[slot, part])
            for part in range(2)
        ]

    def strain_spectra(row):
        held = [spectra_ref[tile, pl.ds(row, many, stride=each), :] for tile in range(tiles)]
        held.append(jnp.broadcast_to(held[-1][:, LANES - 1 :], held[-1].shape))
        per_block = BLOCK // LANES
        span = BLOCK + LANES
        for blk in range(blocks):
            wide = jnp.concatenate(held[blk * per_block : (blk + 1) * per_block + 1], axis=1)
            moved = pltpu.roll(wide, span - meta_ref[blk], 1)[:, :BLOCK]
            yield (moved - wide[:, :BLOCK]).astype(jnp.bfloat16)

    def prepare(f, to_ref):
        for blk, (real, imag) in enumerate(zip(strain_spectra(f), strain_spectra(bins + f), strict=True)):
            to_ref[blk, :many, :BLOCK] = real
            to_ref[blk, many:, :BLOCK] = imag
            to_ref[blk, :many, BLOCK:] = imag
            to_ref[blk, many:, BLOCK:] = -real

    def multiply(f, from_ref):
        slot = lax.rem(f, slots)

        @pl.when(f >= slots)
        def _():
            for c in copies(f - slots, slot):
                c.wait()

        for blk in range(blocks):
            left = from_ref[blk, :, :BLOCK]
            for k in range(PARTNERS):
                tile = lax.dot_general(
                    left,
                    from_ref[blk + meta_ref[blocks * (1 + k) + blk]],
                    (((0,), (0,)), ((), ())),
                    preferred_element_type=jnp.float32,
                )
                if scale != 1.0:
                    tile = tile * scale
                buf_ref[slot, 0, blk, k] = tile[:, :BLOCK].astype(jnp.bfloat16)
                buf_ref[slot, 1, blk, k] = tile[:, BLOCK:].astype(jnp.bfloat16)
        for c in copies(f, slot):
            c.start()

    def step(i, carry):
        prepare(2 * i + 1, odd_ref)
        multiply(2 * i, even_ref)
        prepare(lax.rem(2 * i + 2, bins), even_ref)
        multiply(2 * i + 1, odd_ref)
        return carry

    prepare(0, even_ref)
    lax.fori_loop(0, bins // 2, step, 0)
    for f in range(bins - slots, bins):
        for c in copies(f, f % slots):
            c.wait()


def gram(count, snaps, scale, meta, base, early, own, sib):
    half = early[0].shape[0]
    bins = base.shape[0] // 4
    blocks = 2 * half * LANES // BLOCK
    total = count * snaps * 2 * bins
    slots = 4
    vmem, smem = pl.BlockSpec(memory_space=pltpu.VMEM), pl.BlockSpec(memory_space=pltpu.SMEM)
    return pl.pallas_call(
        functools.partial(gram_kernel, len(early) // 2, snaps, scale, slots),
        in_specs=[smem] + [vmem] * (1 + len(early) + 4),
        out_specs=pl.BlockSpec(memory_space=pltpu.HBM),
        out_shape=jax.ShapeDtypeStruct((2, bins, blocks, PARTNERS, BLOCK, BLOCK), jnp.bfloat16),
        scratch_shapes=[
            pltpu.VMEM((2 * half, total, LANES), jnp.float32),
            pltpu.VMEM((blocks, 2 * count * snaps, 2 * BLOCK), jnp.bfloat16),
            pltpu.VMEM((blocks, 2 * count * snaps, 2 * BLOCK), jnp.bfloat16),
            pltpu.VMEM((slots, 2, blocks, PARTNERS, BLOCK, BLOCK), jnp.bfloat16),
            pltpu.SemaphoreType.DMA((slots, 2)),
        ],
        compiler_params=pltpu.CompilerParams(vmem_limit_bytes=24 << 20),
        name="gram",
    )(meta, base, *early, *own, *sib)


def on_device_ring(optical_phase, gauge_length, snap_starts, partner_offsets):
    count = lax.axis_size("gx")
    pair_devices = lax.axis_size("gy")
    rows_local = optical_phase.shape[0]
    bins_dev = BINS // (count * pair_devices)
    snaps = snap_starts.shape[0]
    order = ring_order(count)
    ahead = [(order[i], order[(i + 1) % count]) for i in range(count)]
    back = [(b, a) for a, b in ahead]

    scale = 1.0 / math.sqrt(count * snaps)
    root = math.sqrt(scale)
    if math.frexp(root)[0] == 0.5:
        fold, scale = root, 1.0
    else:
        fold = 1.0

    cores = lax.axis_index("gy") ^ jnp.arange(pair_devices, dtype=jnp.int32)
    first_bin = (lax.axis_index("gx") * pair_devices + cores) * bins_dev
    bin_index = (first_bin[:, None] + jnp.arange(bins_dev, dtype=jnp.int32)[None, :]).reshape(-1)
    fourier = fourier_table(bin_index, 2 * BINS).astype(jnp.float32) * (taper_window() * fold)
    base = fourier.astype(jnp.bfloat16).astype(jnp.float32).reshape(2, pair_devices, bins_dev, SNAP_LEN)
    base = jnp.transpose(base, (1, 0, 2, 3)).reshape(2 * pair_devices * bins_dev, SNAP_LEN)
    base = jnp.pad(base, ((0, 0), (0, SNAP_LEN)))

    def exchange(x):
        return lax.ppermute(x, "gy", [(0, 1), (1, 0)])

    def tie(*xs):
        return lax.optimization_barrier(xs)

    def spectra(*stretches):
        return spectra_group(snaps, base, stretches)

    def onward(f, b):
        return lax.ppermute(f, "gx", ahead), lax.ppermute(b, "gx", back)

    half_rows = rows_local // 2
    half = optical_phase.shape[1]
    extra = snap_starts.astype(optical_phase.dtype)[:, None, None]
    extra = jnp.broadcast_to(extra, (snaps, 8 // snaps, half)).reshape(8, half)
    f1, b1 = onward(optical_phase, optical_phase)
    ef, eb = lax.ppermute(extra, "gx", ahead), lax.ppermute(extra, "gx", back)
    f1, b1 = jnp.concatenate([f1, ef]), jnp.concatenate([b1, eb])
    own = jnp.concatenate([optical_phase, extra])
    meta = jnp.concatenate([gauge_length, partner_offsets.T.reshape(-1)])
    f1, own, base, meta = tie(f1, own, base, meta)
    f2, b2 = onward(f1, b1)
    near1, far1 = spectra(own, f1, b1)
    f3, b3 = onward(f2, b2)
    other1 = exchange(far1)
    near2, far2 = spectra(f2, b2)
    f4, b4 = onward(f3[:half_rows], b3[half_rows:])
    other2 = exchange(far2)
    near3, far3 = spectra(f3, b3)
    own4, sib4 = (f4, b4), (exchange(f4), exchange(b4))
    other3 = exchange(far3)
    early = (near1, other1, near2, other2, near3, other3)
    return gram(count, snaps, scale, meta, base, early, own4, sib4)


def strain_blocks(extended, gauges):
    blocks = gauges.shape[0]
    block_first = jnp.arange(blocks, dtype=jnp.int32) * BLOCK

    def pick_block(column):
        return lax.dynamic_slice_in_dim(extended, column, BLOCK, 1)

    shifted = jax.vmap(pick_block)(block_first + gauges)
    initial = extended[:, : blocks * BLOCK].reshape(extended.shape[0], blocks, BLOCK)
    return shifted - jnp.transpose(initial, (1, 0, 2))


def tapered_segments(strain, start_rows):
    window = taper_window()

    def segment_at(row_start):
        return lax.dynamic_slice_in_dim(strain, row_start, SNAP_LEN, 1)

    segments = jax.vmap(segment_at)(start_rows)
    return (window[None, None, :, None] * segments).astype(jnp.bfloat16)


def spectra_for(tapered, bin_index):
    fourier = fourier_table(bin_index, 2 * BINS)
    spectrum = jnp.einsum("cft,sbtj->scfbj", fourier, tapered, preferred_element_type=jnp.float32)
    shape_out = spectrum.shape
    return spectrum.astype(jnp.bfloat16).reshape(
        shape_out[0], 2, shape_out[2], shape_out[3] * BLOCK
    )


def on_device(optical_phase, gauge_length, snap_starts, partner_offsets):
    time_devices = lax.axis_size("gx")
    pair_devices = lax.axis_size("gy")
    pair_index = lax.axis_index("gy")
    rows_local = optical_phase.shape[0]
    bins_dev = BINS // (time_devices * pair_devices)
    whole_phase = lax.all_gather(optical_phase, "gy", axis=1, tiled=True)
    edge_cols = jnp.broadcast_to(whole_phase[:, -1:], (rows_local, GAUGE_MAX))
    extended = jnp.concatenate([whole_phase, edge_cols], axis=1).astype(jnp.float32)
    strain = strain_blocks(extended, gauge_length)
    tapered = tapered_segments(strain, snap_starts)
    owner_slot = jnp.arange(time_devices * bins_dev, dtype=jnp.int32)
    bin_index = (
        owner_slot // bins_dev * pair_devices + pair_index
    ) * bins_dev + owner_slot % bins_dev
    spectra = spectra_for(tapered, bin_index)
    gathered = lax.all_to_all(spectra, "gx", split_axis=2, concat_axis=0, tiled=True)
    snaps_all = gathered.shape[0]
    blocks_all = gathered.shape[3] // BLOCK
    spectra_blocks = gathered.reshape(snaps_all, 2, bins_dev, blocks_all, BLOCK)
    partners = jnp.arange(blocks_all, dtype=jnp.int32)[:, None] + partner_offsets
    partner_data = jnp.take(spectra_blocks, partners.reshape(-1), axis=3)
    partner_data = partner_data.reshape(snaps_all, 2, bins_dev, blocks_all, PARTNERS, BLOCK)
    swapped = jnp.stack([partner_data[:, 1], -partner_data[:, 0]], axis=1)
    stacked = jnp.stack([partner_data, swapped])
    gram_tile = jnp.einsum(
        "scfbi,pscfbkj->pfbkij", spectra_blocks, stacked, preferred_element_type=jnp.float32
    )
    return (gram_tile * (1.0 / math.sqrt(snaps_all))).astype(jnp.bfloat16)


def solution(mesh):
    in_specs = (P(("fiber", "gx"), "gy"), P("fiber"), P(("fiber", "gx")), P("fiber", None))
    out_specs = P("fiber", ("gx", "gy"), None, None, None, None)

    def body(optical_phase, gauge_length, snap_starts, partner_offsets):
        ring = lax.axis_size("gx") == 8 and lax.axis_size("gy") == 2 and snap_starts.shape[0] == 2
        plan = on_device_ring if ring else on_device
        return plan(optical_phase, gauge_length, snap_starts, partner_offsets)

    return jax.shard_map(body, mesh=mesh, in_specs=in_specs, out_specs=out_specs, check_vma=False)
```

```python
import functools
import math

import jax
import jax.numpy as jnp
from jax import lax
from jax.experimental import pallas as pl
from jax.experimental.pallas import tpu as pltpu
from jax.sharding import PartitionSpec as P


BINS = 256
BLOCK = 256
SNAP_LEN = 128
GAUGE_MAX = 16
PARTNERS = 2
LANES = 128


def fourier_table(bin_index, total_len):
    sample = jnp.arange(SNAP_LEN, dtype=jnp.int32)
    product = bin_index[:, None] * sample[None, :] % total_len
    angles = 2.0 * math.pi / total_len * product.astype(jnp.float32)
    factor = 1.0 / math.sqrt(SNAP_LEN)
    return jnp.stack([jnp.cos(angles) * factor, -jnp.sin(angles) * factor]).astype(jnp.bfloat16)


def taper_window():
    sample = jnp.arange(SNAP_LEN, dtype=jnp.int32).astype(jnp.float32)
    return 0.5 - 0.5 * jnp.cos(2.0 * math.pi / SNAP_LEN * sample)


def ring_order(count):
    return [*range(0, count, 2), *range(count - 1, 0, -2)]


def starts_in(extra, snaps):
    values = extra.astype(jnp.float32).astype(jnp.int32)
    return [values[n * (8 // snaps), 0] for n in range(snaps)]


def shifted_table(base, starts):
    return jnp.concatenate([pltpu.roll(base, start, 1) for start in starts], axis=0).astype(jnp.bfloat16)


def spectra_kernel(snaps, base_ref, *refs):
    *stretches, near_ref, far_ref = refs
    rows = stretches[0].shape[0] - 8
    tiles = near_ref.shape[0]
    each = base_ref.shape[0] // 2
    for n, ref in enumerate(stretches):
        table = shifted_table(base_ref[...], starts_in(ref[rows:, :], snaps))[:, :rows]
        out = jnp.dot(table, ref[:rows, :], preferred_element_type=jnp.float32)
        for snap in range(snaps):
            for part, to_ref in enumerate((near_ref, far_ref)):
                at = (snap * 2 + part) * each
                to = (n * snaps + snap) * each
                for tile in range(tiles):
                    to_ref[tile, to : to + each, :] = out[at : at + each, tile * LANES : (tile + 1) * LANES]


def spectra_group(snaps, base, stretches):
    half = stretches[0].shape[1]
    each = base.shape[0] // 2
    count = len(stretches)
    shape = jax.ShapeDtypeStruct((half // LANES, count * snaps * each, LANES), jnp.float32)
    vmem = pl.BlockSpec(memory_space=pltpu.VMEM)
    return pl.pallas_call(
        functools.partial(spectra_kernel, snaps),
        in_specs=[vmem] * (1 + count),
        out_specs=(vmem, vmem),
        out_shape=(shape, shape),
        cost_estimate=pl.CostEstimate(
            flops=count * 100_000_000, bytes_accessed=count * 400_000, transcendentals=0
        ),
        compiler_params=pltpu.CompilerParams(vmem_limit_bytes=8 << 20),
        name="spectra",
    )(base, *stretches)


def gram_kernel(groups, snaps, scale, slots, meta_ref, base_ref, *refs):
    early = refs[: 2 * groups]
    own0, own1, sib0, sib1 = refs[2 * groups : 2 * groups + 4]
    out_ref, spectra_ref, *operands, buf_ref, sems = refs[2 * groups + 4 :]
    side = lax.axis_index("gy")
    bins = out_ref.shape[1]
    tiles, total, _ = spectra_ref.shape
    half = tiles // 2
    blocks = tiles * LANES // BLOCK
    each = 2 * bins
    many = total // each
    rows = own0.shape[0] + own1.shape[0] - 8
    cut = own0.shape[0]

    done = 0
    for n, ref in enumerate(early):
        side_of = side if n % 2 == 0 else 1 - side
        for tile in range(half):
            spectra_ref[side_of * half + tile, done : done + ref.shape[1], :] = ref[tile]
        done += ref.shape[1] * (n % 2)
    table = shifted_table(base_ref[:each, :], starts_in(own1[rows - cut :, :], snaps))[:, :rows]
    for core, (lower, upper) in enumerate(((own0, own1), (sib0, sib1))):
        phase = jnp.concatenate([lower[...], upper[: rows - cut, :]], axis=0)
        out = jnp.dot(table, phase, preferred_element_type=jnp.float32)
        side_of = side if core == 0 else 1 - side
        for tile in range(half):
            spectra_ref[side_of * half + tile, done:, :] = out[:, tile * LANES : (tile + 1) * LANES]

    def copies(f, slot):
        return [
            pltpu.make_async_copy(buf_ref.at[slot, part], out_ref.at[part, f], sems.at[slot, part])
            for part in range(2)
        ]

    def strain_spectra(row):
        held = [spectra_ref[tile, pl.ds(row, many, stride=each), :] for tile in range(tiles)]
        held.append(jnp.broadcast_to(held[-1][:, LANES - 1 :], held[-1].shape))
        per_block = BLOCK // LANES
        span = BLOCK + LANES
        for blk in range(blocks):
            wide = jnp.concatenate(held[blk * per_block : (blk + 1) * per_block + 1], axis=1)
            moved = pltpu.roll(wide, span - meta_ref[blk], 1)[:, :BLOCK]
            yield (moved - wide[:, :BLOCK]).astype(jnp.bfloat16)

    def prepare(f, to_ref):
        for blk, (real, imag) in enumerate(zip(strain_spectra(f), strain_spectra(bins + f), strict=True)):
            to_ref[blk, :many, :BLOCK] = real
            to_ref[blk, many:, :BLOCK] = imag
            to_ref[blk, :many, BLOCK:] = imag
            to_ref[blk, many:, BLOCK:] = -real

    def multiply(f, from_ref):
        slot = lax.rem(f, slots)
        for blk in range(blocks):
            left = from_ref[blk, :, :BLOCK]
            for k in range(PARTNERS):
                tile = lax.dot_general(
                    left,
                    from_ref[meta_ref[blocks * (1 + k) + blk]],
                    (((0,), (0,)), ((), ())),
                    preferred_element_type=jnp.float32,
                )
                if scale != 1.0:
                    tile = tile * scale
                buf_ref[slot, 0, blk, k] = tile[:, :BLOCK].astype(jnp.bfloat16)
                buf_ref[slot, 1, blk, k] = tile[:, BLOCK:].astype(jnp.bfloat16)
        for c in copies(f, slot):
            c.start()

    def free(f):
        @pl.when(f >= slots)
        def _():
            for n in (f, f + 1):
                for c in copies(n - slots, lax.rem(n, slots)):
                    c.wait()

    def step(i, carry):
        f = 4 * i
        for n in (0, 2):
            free(f + n)
            multiply(f + n, operands[n])
            prepare(lax.rem(f + n + 2, bins), operands[2 - n])
            multiply(f + n + 1, operands[n + 1])
            prepare(lax.rem(f + n + 3, bins), operands[3 - n])
        return carry

    prepare(0, operands[0])
    prepare(1, operands[1])
    lax.fori_loop(0, bins // 4, step, 0)
    for f in range(bins - slots, bins):
        for c in copies(f, f % slots):
            c.wait()


def gram(count, snaps, scale, meta, base, early, own, sib):
    half = early[0].shape[0]
    bins = base.shape[0] // 4
    blocks = 2 * half * LANES // BLOCK
    total = count * snaps * 2 * bins
    slots = 4
    vmem, smem = pl.BlockSpec(memory_space=pltpu.VMEM), pl.BlockSpec(memory_space=pltpu.SMEM)
    return pl.pallas_call(
        functools.partial(gram_kernel, len(early) // 2, snaps, scale, slots),
        in_specs=[smem] + [vmem] * (1 + len(early) + 4),
        out_specs=pl.BlockSpec(memory_space=pltpu.HBM),
        out_shape=jax.ShapeDtypeStruct((2, bins, blocks, PARTNERS, BLOCK, BLOCK), jnp.bfloat16),
        scratch_shapes=[
            pltpu.VMEM((2 * half, total, LANES), jnp.float32),
            *[pltpu.VMEM((blocks, 2 * count * snaps, 2 * BLOCK), jnp.bfloat16)] * 4,
            pltpu.VMEM((slots, 2, blocks, PARTNERS, BLOCK, BLOCK), jnp.bfloat16),
            pltpu.SemaphoreType.DMA((slots, 2)),
        ],
        compiler_params=pltpu.CompilerParams(vmem_limit_bytes=24 << 20),
        name="gram",
    )(meta, base, *early, *own, *sib)


def on_device_ring(optical_phase, gauge_length, snap_starts, partner_offsets):
    count = lax.axis_size("gx")
    pair_devices = lax.axis_size("gy")
    rows_local = optical_phase.shape[0]
    bins_dev = BINS // (count * pair_devices)
    snaps = snap_starts.shape[0]
    order = ring_order(count)
    ahead = [(order[i], order[(i + 1) % count]) for i in range(count)]
    back = [(b, a) for a, b in ahead]

    scale = 1.0 / math.sqrt(count * snaps)
    root = math.sqrt(scale)
    if math.frexp(root)[0] == 0.5:
        fold, scale = root, 1.0
    else:
        fold = 1.0

    cores = lax.axis_index("gy") ^ jnp.arange(pair_devices, dtype=jnp.int32)
    first_bin = (lax.axis_index("gx") * pair_devices + cores) * bins_dev
    bin_index = (first_bin[:, None] + jnp.arange(bins_dev, dtype=jnp.int32)[None, :]).reshape(-1)
    fourier = fourier_table(bin_index, 2 * BINS).astype(jnp.float32) * (taper_window() * fold)
    base = fourier.astype(jnp.bfloat16).astype(jnp.float32).reshape(2, pair_devices, bins_dev, SNAP_LEN)
    base = jnp.transpose(base, (1, 0, 2, 3)).reshape(2 * pair_devices * bins_dev, SNAP_LEN)
    base = jnp.pad(base, ((0, 0), (0, SNAP_LEN)))

    def exchange(x):
        return lax.ppermute(x, "gy", [(0, 1), (1, 0)])

    def tie(*xs):
        return lax.optimization_barrier(xs)

    def spectra(*stretches):
        return spectra_group(snaps, base, stretches)

    def onward(f, b):
        f = lax.ppermute(f, "gx", ahead)
        b = lax.ppermute(b, "gx", back)
        return f, b

    half_rows = rows_local // 2
    half = optical_phase.shape[1]
    extra = snap_starts.astype(optical_phase.dtype)[:, None, None]
    extra = jnp.broadcast_to(extra, (snaps, 8 // snaps, half)).reshape(8, half)
    f1, b1 = onward(optical_phase, optical_phase)
    ef, eb = lax.ppermute(extra, "gx", ahead), lax.ppermute(extra, "gx", back)
    f1, b1 = jnp.concatenate([f1, ef]), jnp.concatenate([b1, eb])
    own = jnp.concatenate([optical_phase, extra])
    f2, b2 = onward(f1, b1)
    near1, far1 = spectra(own, f1, b1)
    f2, gauges, offsets = tie(f2, gauge_length, partner_offsets)
    partners = offsets.T + jnp.arange(offsets.shape[0], dtype=jnp.int32)[None, :]
    meta = jnp.concatenate([gauges, partners.reshape(-1)])
    f3, b3 = onward(f2, b2)
    other1 = exchange(far1)
    near2, far2 = spectra(f2, b2)
    f4, b4 = onward(f3[:half_rows], b3[half_rows:])
    other2 = exchange(far2)
    near3, far3 = spectra(f3, b3)
    s_b4 = exchange(b4)
    s_f4 = exchange(f4)
    other3 = exchange(far3)
    early = (near1, other1, near2, other2, near3, other3)
    return gram(count, snaps, scale, meta, base, early, (f4, b4), (s_f4, s_b4))


def strain_blocks(extended, gauges):
    blocks = gauges.shape[0]
    block_first = jnp.arange(blocks, dtype=jnp.int32) * BLOCK

    def pick_block(column):
        return lax.dynamic_slice_in_dim(extended, column, BLOCK, 1)

    shifted = jax.vmap(pick_block)(block_first + gauges)
    initial = extended[:, : blocks * BLOCK].reshape(extended.shape[0], blocks, BLOCK)
    return shifted - jnp.transpose(initial, (1, 0, 2))


def tapered_segments(strain, start_rows):
    window = taper_window()

    def segment_at(row_start):
        return lax.dynamic_slice_in_dim(strain, row_start, SNAP_LEN, 1)

    segments = jax.vmap(segment_at)(start_rows)
    return (window[None, None, :, None] * segments).astype(jnp.bfloat16)


def spectra_for(tapered, bin_index):
    fourier = fourier_table(bin_index, 2 * BINS)
    spectrum = jnp.einsum("cft,sbtj->scfbj", fourier, tapered, preferred_element_type=jnp.float32)
    shape_out = spectrum.shape
    return spectrum.astype(jnp.bfloat16).reshape(
        shape_out[0], 2, shape_out[2], shape_out[3] * BLOCK
    )


def on_device(optical_phase, gauge_length, snap_starts, partner_offsets):
    time_devices = lax.axis_size("gx")
    pair_devices = lax.axis_size("gy")
    pair_index = lax.axis_index("gy")
    rows_local = optical_phase.shape[0]
    bins_dev = BINS // (time_devices * pair_devices)
    whole_phase = lax.all_gather(optical_phase, "gy", axis=1, tiled=True)
    edge_cols = jnp.broadcast_to(whole_phase[:, -1:], (rows_local, GAUGE_MAX))
    extended = jnp.concatenate([whole_phase, edge_cols], axis=1).astype(jnp.float32)
    strain = strain_blocks(extended, gauge_length)
    tapered = tapered_segments(strain, snap_starts)
    owner_slot = jnp.arange(time_devices * bins_dev, dtype=jnp.int32)
    bin_index = (
        owner_slot // bins_dev * pair_devices + pair_index
    ) * bins_dev + owner_slot % bins_dev
    spectra = spectra_for(tapered, bin_index)
    gathered = lax.all_to_all(spectra, "gx", split_axis=2, concat_axis=0, tiled=True)
    snaps_all = gathered.shape[0]
    blocks_all = gathered.shape[3] // BLOCK
    spectra_blocks = gathered.reshape(snaps_all, 2, bins_dev, blocks_all, BLOCK)
    partners = jnp.arange(blocks_all, dtype=jnp.int32)[:, None] + partner_offsets
    partner_data = jnp.take(spectra_blocks, partners.reshape(-1), axis=3)
    partner_data = partner_data.reshape(snaps_all, 2, bins_dev, blocks_all, PARTNERS, BLOCK)
    swapped = jnp.stack([partner_data[:, 1], -partner_data[:, 0]], axis=1)
    stacked = jnp.stack([partner_data, swapped])
    gram_tile = jnp.einsum(
        "scfbi,pscfbkj->pfbkij", spectra_blocks, stacked, preferred_element_type=jnp.float32
    )
    return (gram_tile * (1.0 / math.sqrt(snaps_all))).astype(jnp.bfloat16)


def solution(mesh):
    in_specs = (P(("fiber", "gx"), "gy"), P("fiber"), P(("fiber", "gx")), P("fiber", None))
    out_specs = P("fiber", ("gx", "gy"), None, None, None, None)

    def body(optical_phase, gauge_length, snap_starts, partner_offsets):
        ring = lax.axis_size("gx") == 8 and lax.axis_size("gy") == 2 and snap_starts.shape[0] == 2
        plan = on_device_ring if ring else on_device
        return plan(optical_phase, gauge_length, snap_starts, partner_offsets)

    return jax.shard_map(body, mesh=mesh, in_specs=in_specs, out_specs=out_specs, check_vma=False)
```

```python
import functools
import math

import jax
import jax.numpy as jnp
from jax import lax
from jax.experimental import pallas as pl
from jax.experimental.pallas import tpu as pltpu
from jax.sharding import PartitionSpec as P


BINS = 256
BLOCK = 256
SNAP_LEN = 128
GAUGE_MAX = 16
PARTNERS = 2
LANES = 128


def fourier_table(bin_index, total_len):
    sample = jnp.arange(SNAP_LEN, dtype=jnp.int32)
    product = bin_index[:, None] * sample[None, :] % total_len
    angles = 2.0 * math.pi / total_len * product.astype(jnp.float32)
    factor = 1.0 / math.sqrt(SNAP_LEN)
    return jnp.stack([jnp.cos(angles) * factor, -jnp.sin(angles) * factor]).astype(jnp.bfloat16)


def taper_window():
    sample = jnp.arange(SNAP_LEN, dtype=jnp.int32).astype(jnp.float32)
    return 0.5 - 0.5 * jnp.cos(2.0 * math.pi / SNAP_LEN * sample)


def ring_order(count):
    return [*range(0, count, 2), *range(count - 1, 0, -2)]


def starts_in(extra, snaps):
    values = extra.astype(jnp.float32).astype(jnp.int32)
    return [values[n * (8 // snaps), 0] for n in range(snaps)]


def shifted_table(base, starts):
    return jnp.concatenate([pltpu.roll(base, start, 1) for start in starts], axis=0).astype(jnp.bfloat16)


def spectra_kernel(snaps, base_ref, *refs):
    *stretches, near_ref, far_ref = refs
    rows = stretches[0].shape[0] - 8
    tiles = near_ref.shape[0]
    each = base_ref.shape[0] // 2
    for n, ref in enumerate(stretches):
        table = shifted_table(base_ref[...], starts_in(ref[rows:, :], snaps))[:, :rows]
        out = jnp.dot(table, ref[:rows, :], preferred_element_type=jnp.float32)
        for snap in range(snaps):
            for part, to_ref in enumerate((near_ref, far_ref)):
                at = (snap * 2 + part) * each
                to = (n * snaps + snap) * each
                for tile in range(tiles):
                    to_ref[tile, to : to + each, :] = out[at : at + each, tile * LANES : (tile + 1) * LANES]


def spectra_group(snaps, base, stretches):
    half = stretches[0].shape[1]
    each = base.shape[0] // 2
    count = len(stretches)
    shape = jax.ShapeDtypeStruct((half // LANES, count * snaps * each, LANES), jnp.float32)
    vmem = pl.BlockSpec(memory_space=pltpu.VMEM)
    return pl.pallas_call(
        functools.partial(spectra_kernel, snaps),
        in_specs=[vmem] * (1 + count),
        out_specs=(vmem, vmem),
        out_shape=(shape, shape),
        cost_estimate=pl.CostEstimate(
            flops=count * 100_000_000, bytes_accessed=count * 400_000, transcendentals=0
        ),
        compiler_params=pltpu.CompilerParams(vmem_limit_bytes=8 << 20),
        name="spectra",
    )(base, *stretches)


def gram_kernel(groups, snaps, scale, slots, meta_ref, base_ref, *refs):
    early = refs[: 2 * groups]
    own0, own1, sib0, sib1 = refs[2 * groups : 2 * groups + 4]
    out_ref, spectra_ref, *operands, buf_ref, sems = refs[2 * groups + 4 :]
    side = lax.axis_index("gy")
    bins = out_ref.shape[1]
    tiles, total, _ = spectra_ref.shape
    half = tiles // 2
    blocks = tiles * LANES // BLOCK
    each = 2 * bins
    many = total // each
    rows = own0.shape[0] + own1.shape[0] - 8
    cut = own0.shape[0]

    done = 0
    for n, ref in enumerate(early):
        side_of = side if n % 2 == 0 else 1 - side
        for tile in range(half):
            spectra_ref[side_of * half + tile, done : done + ref.shape[1], :] = ref[tile]
        done += ref.shape[1] * (n % 2)
    table = shifted_table(base_ref[:each, :], starts_in(own1[rows - cut :, :], snaps))[:, :rows]
    for core, (lower, upper) in enumerate(((own0, own1), (sib0, sib1))):
        phase = jnp.concatenate([lower[...], upper[: rows - cut, :]], axis=0)
        out = jnp.dot(table, phase, preferred_element_type=jnp.float32)
        side_of = side if core == 0 else 1 - side
        for tile in range(half):
            spectra_ref[side_of * half + tile, done:, :] = out[:, tile * LANES : (tile + 1) * LANES]

    def copies(f, slot):
        return [
            pltpu.make_async_copy(buf_ref.at[slot, part, blk], out_ref.at[part, f, blk], sems.at[slot, part, blk])
            for blk in range(blocks)
            for part in range(2)
        ]

    def strain_spectra(row):
        held = [spectra_ref[tile, pl.ds(row, many, stride=each), :] for tile in range(tiles)]
        held.append(jnp.broadcast_to(held[-1][:, LANES - 1 :], held[-1].shape))
        per_block = BLOCK // LANES
        span = BLOCK + LANES
        for blk in range(blocks):
            wide = jnp.concatenate(held[blk * per_block : (blk + 1) * per_block + 1], axis=1)
            moved = pltpu.roll(wide, span - meta_ref[blk], 1)[:, :BLOCK]
            yield (moved - wide[:, :BLOCK]).astype(jnp.bfloat16)

    def prepare(f, to_ref):
        for blk, (real, imag) in enumerate(zip(strain_spectra(f), strain_spectra(bins + f), strict=True)):
            to_ref[blk, :many, :BLOCK] = real
            to_ref[blk, many:, :BLOCK] = imag
            to_ref[blk, :many, BLOCK:] = imag
            to_ref[blk, many:, BLOCK:] = -real

    def multiply(f, from_ref):
        slot = lax.rem(f, slots)
        for blk in range(blocks):
            left = from_ref[blk, :, :BLOCK]
            for k in range(PARTNERS):
                tile = lax.dot_general(
                    left,
                    from_ref[meta_ref[blocks * (1 + k) + blk]],
                    (((0,), (0,)), ((), ())),
                    preferred_element_type=jnp.float32,
                )
                if scale != 1.0:
                    tile = tile * scale
                buf_ref[slot, 0, blk, k] = tile[:, :BLOCK].astype(jnp.bfloat16)
                buf_ref[slot, 1, blk, k] = tile[:, BLOCK:].astype(jnp.bfloat16)
            for c in copies(f, slot)[2 * blk : 2 * blk + 2]:
                c.start()

    def free(f):
        @pl.when(f >= slots)
        def _():
            for n in (f, f + 1):
                for c in copies(n - slots, lax.rem(n, slots)):
                    c.wait()

    def step(i, carry):
        f = 4 * i
        for n in (0, 2):
            free(f + n)
            multiply(f + n, operands[n])
            prepare(lax.rem(f + n + 2, bins), operands[2 - n])
            multiply(f + n + 1, operands[n + 1])
            prepare(lax.rem(f + n + 3, bins), operands[3 - n])
        return carry

    prepare(0, operands[0])
    prepare(1, operands[1])
    lax.fori_loop(0, bins // 4, step, 0)
    for f in range(bins - slots, bins):
        for c in copies(f, f % slots):
            c.wait()


def gram(count, snaps, scale, meta, base, early, own, sib):
    half = early[0].shape[0]
    bins = base.shape[0] // 4
    blocks = 2 * half * LANES // BLOCK
    total = count * snaps * 2 * bins
    slots = 4
    vmem, smem = pl.BlockSpec(memory_space=pltpu.VMEM), pl.BlockSpec(memory_space=pltpu.SMEM)
    return pl.pallas_call(
        functools.partial(gram_kernel, len(early) // 2, snaps, scale, slots),
        in_specs=[smem] + [vmem] * (1 + len(early) + 4),
        out_specs=pl.BlockSpec(memory_space=pltpu.HBM),
        out_shape=jax.ShapeDtypeStruct((2, bins, blocks, PARTNERS, BLOCK, BLOCK), jnp.bfloat16),
        scratch_shapes=[
            pltpu.VMEM((2 * half, total, LANES), jnp.float32),
            *[pltpu.VMEM((blocks, 2 * count * snaps, 2 * BLOCK), jnp.bfloat16)] * 4,
            pltpu.VMEM((slots, 2, blocks, PARTNERS, BLOCK, BLOCK), jnp.bfloat16),
            pltpu.SemaphoreType.DMA((slots, 2, blocks)),
        ],
        compiler_params=pltpu.CompilerParams(vmem_limit_bytes=24 << 20),
        name="gram",
    )(meta, base, *early, *own, *sib)


def on_device_ring(optical_phase, gauge_length, snap_starts, partner_offsets):
    count = lax.axis_size("gx")
    pair_devices = lax.axis_size("gy")
    rows_local = optical_phase.shape[0]
    bins_dev = BINS // (count * pair_devices)
    snaps = snap_starts.shape[0]
    order = ring_order(count)

    scale = 1.0 / math.sqrt(count * snaps)
    root = math.sqrt(scale)
    if math.frexp(root)[0] == 0.5:
        fold, scale = root, 1.0
    else:
        fold = 1.0

    cores = lax.axis_index("gy") ^ jnp.arange(pair_devices, dtype=jnp.int32)
    first_bin = (lax.axis_index("gx") * pair_devices + cores) * bins_dev
    bin_index = (first_bin[:, None] + jnp.arange(bins_dev, dtype=jnp.int32)[None, :]).reshape(-1)
    fourier = fourier_table(bin_index, 2 * BINS).astype(jnp.float32) * (taper_window() * fold)
    base = fourier.astype(jnp.bfloat16).astype(jnp.float32).reshape(2, pair_devices, bins_dev, SNAP_LEN)
    base = jnp.transpose(base, (1, 0, 2, 3)).reshape(2 * pair_devices * bins_dev, SNAP_LEN)
    base = jnp.pad(base, ((0, 0), (0, SNAP_LEN)))

    def exchange(x):
        return lax.ppermute(x, "gy", [(0, 1), (1, 0)])

    def tie(*xs):
        return lax.optimization_barrier(xs)

    def spectra(*stretches):
        return spectra_group(snaps, base, stretches)

    def moved(x, places):
        return lax.ppermute(x, "gx", [(order[i], order[(i + places) % count]) for i in range(count)])

    def onward(f, b, places=1):
        f = moved(f, places)
        b = moved(b, -places)
        return f, b

    half_rows = rows_local // 2
    half = optical_phase.shape[1]
    extra = snap_starts.astype(optical_phase.dtype)[:, None, None]
    extra = jnp.broadcast_to(extra, (snaps, 8 // snaps, half)).reshape(8, half)
    f1, b1 = onward(optical_phase, optical_phase)
    ef, eb = onward(extra, extra)
    f1, b1 = jnp.concatenate([f1, ef]), jnp.concatenate([b1, eb])
    own = jnp.concatenate([optical_phase, extra])
    f2, b2 = onward(f1, b1)
    near1, far1 = spectra(own, f1, b1)
    near1, gauges, offsets = tie(near1, gauge_length, partner_offsets)
    partners = offsets.T + jnp.arange(offsets.shape[0], dtype=jnp.int32)[None, :]
    meta = jnp.concatenate([gauges, partners.reshape(-1)])
    other1 = exchange(far1)
    f3, b3 = onward(f2, b2)
    f4, b4 = onward(f2[:half_rows], b2[half_rows:], 2)
    near2, far2 = spectra(f2, b2)
    other2 = exchange(far2)
    b4, meta = tie(b4, meta)
    near3, far3 = spectra(f3, b3)
    s_b4 = exchange(b4)
    s_f4 = exchange(f4)
    other3 = exchange(far3)
    early = (near1, other1, near2, other2, near3, other3)
    return gram(count, snaps, scale, meta, base, early, (f4, b4), (s_f4, s_b4))


def strain_blocks(extended, gauges):
    blocks = gauges.shape[0]
    block_first = jnp.arange(blocks, dtype=jnp.int32) * BLOCK

    def pick_block(column):
        return lax.dynamic_slice_in_dim(extended, column, BLOCK, 1)

    shifted = jax.vmap(pick_block)(block_first + gauges)
    initial = extended[:, : blocks * BLOCK].reshape(extended.shape[0], blocks, BLOCK)
    return shifted - jnp.transpose(initial, (1, 0, 2))


def tapered_segments(strain, start_rows):
    window = taper_window()

    def segment_at(row_start):
        return lax.dynamic_slice_in_dim(strain, row_start, SNAP_LEN, 1)

    segments = jax.vmap(segment_at)(start_rows)
    return (window[None, None, :, None] * segments).astype(jnp.bfloat16)


def spectra_for(tapered, bin_index):
    fourier = fourier_table(bin_index, 2 * BINS)
    spectrum = jnp.einsum("cft,sbtj->scfbj", fourier, tapered, preferred_element_type=jnp.float32)
    shape_out = spectrum.shape
    return spectrum.astype(jnp.bfloat16).reshape(
        shape_out[0], 2, shape_out[2], shape_out[3] * BLOCK
    )


def on_device(optical_phase, gauge_length, snap_starts, partner_offsets):
    time_devices = lax.axis_size("gx")
    pair_devices = lax.axis_size("gy")
    pair_index = lax.axis_index("gy")
    rows_local = optical_phase.shape[0]
    bins_dev = BINS // (time_devices * pair_devices)
    whole_phase = lax.all_gather(optical_phase, "gy", axis=1, tiled=True)
    edge_cols = jnp.broadcast_to(whole_phase[:, -1:], (rows_local, GAUGE_MAX))
    extended = jnp.concatenate([whole_phase, edge_cols], axis=1).astype(jnp.float32)
    strain = strain_blocks(extended, gauge_length)
    tapered = tapered_segments(strain, snap_starts)
    owner_slot = jnp.arange(time_devices * bins_dev, dtype=jnp.int32)
    bin_index = (
        owner_slot // bins_dev * pair_devices + pair_index
    ) * bins_dev + owner_slot % bins_dev
    spectra = spectra_for(tapered, bin_index)
    gathered = lax.all_to_all(spectra, "gx", split_axis=2, concat_axis=0, tiled=True)
    snaps_all = gathered.shape[0]
    blocks_all = gathered.shape[3] // BLOCK
    spectra_blocks = gathered.reshape(snaps_all, 2, bins_dev, blocks_all, BLOCK)
    partners = jnp.arange(blocks_all, dtype=jnp.int32)[:, None] + partner_offsets
    partner_data = jnp.take(spectra_blocks, partners.reshape(-1), axis=3)
    partner_data = partner_data.reshape(snaps_all, 2, bins_dev, blocks_all, PARTNERS, BLOCK)
    swapped = jnp.stack([partner_data[:, 1], -partner_data[:, 0]], axis=1)
    stacked = jnp.stack([partner_data, swapped])
    gram_tile = jnp.einsum(
        "scfbi,pscfbkj->pfbkij", spectra_blocks, stacked, preferred_element_type=jnp.float32
    )
    return (gram_tile * (1.0 / math.sqrt(snaps_all))).astype(jnp.bfloat16)


def solution(mesh):
    in_specs = (P(("fiber", "gx"), "gy"), P("fiber"), P(("fiber", "gx")), P("fiber", None))
    out_specs = P("fiber", ("gx", "gy"), None, None, None, None)

    def body(optical_phase, gauge_length, snap_starts, partner_offsets):
        ring = lax.axis_size("gx") == 8 and lax.axis_size("gy") == 2 and snap_starts.shape[0] == 2
        plan = on_device_ring if ring else on_device
        return plan(optical_phase, gauge_length, snap_starts, partner_offsets)

    return jax.shard_map(body, mesh=mesh, in_specs=in_specs, out_specs=out_specs, check_vma=False)
```

```python
import functools
import math

import jax
import jax.numpy as jnp
from jax import lax
from jax.experimental import pallas as pl
from jax.experimental.pallas import tpu as pltpu
from jax.sharding import PartitionSpec as P


BINS = 256
BLOCK = 256
SNAP_LEN = 128
GAUGE_MAX = 16
PARTNERS = 2
LANES = 128


def fourier_table(bin_index, total_len):
    sample = jnp.arange(SNAP_LEN, dtype=jnp.int32)
    product = bin_index[:, None] * sample[None, :] % total_len
    angles = 2.0 * math.pi / total_len * product.astype(jnp.float32)
    factor = 1.0 / math.sqrt(SNAP_LEN)
    return jnp.stack([jnp.cos(angles) * factor, -jnp.sin(angles) * factor]).astype(jnp.bfloat16)


def taper_window():
    sample = jnp.arange(SNAP_LEN, dtype=jnp.int32).astype(jnp.float32)
    return 0.5 - 0.5 * jnp.cos(2.0 * math.pi / SNAP_LEN * sample)


def ring_order(count):
    return [*range(0, count, 2), *range(count - 1, 0, -2)]


def starts_in(extra, snaps):
    values = extra.astype(jnp.float32).astype(jnp.int32)
    return [values[n * (8 // snaps), 0] for n in range(snaps)]


def shifted_table(base, starts):
    return jnp.concatenate([pltpu.roll(base, start, 1) for start in starts], axis=0).astype(jnp.bfloat16)


def spectra_kernel(snaps, base_ref, *refs):
    *stretches, near_ref, far_ref = refs
    rows = stretches[0].shape[0] - 8
    tiles = near_ref.shape[0]
    each = base_ref.shape[0] // 2
    for n, ref in enumerate(stretches):
        table = shifted_table(base_ref[...], starts_in(ref[rows:, :], snaps))[:, :rows]
        out = jnp.dot(table, ref[:rows, :], preferred_element_type=jnp.float32)
        for snap in range(snaps):
            for part, to_ref in enumerate((near_ref, far_ref)):
                at = (snap * 2 + part) * each
                to = (n * snaps + snap) * each
                for tile in range(tiles):
                    to_ref[tile, to : to + each, :] = out[at : at + each, tile * LANES : (tile + 1) * LANES]


def spectra_group(snaps, base, stretches):
    half = stretches[0].shape[1]
    each = base.shape[0] // 2
    count = len(stretches)
    shape = jax.ShapeDtypeStruct((half // LANES, count * snaps * each, LANES), jnp.float32)
    vmem = pl.BlockSpec(memory_space=pltpu.VMEM)
    return pl.pallas_call(
        functools.partial(spectra_kernel, snaps),
        in_specs=[vmem] * (1 + count),
        out_specs=(vmem, vmem),
        out_shape=(shape, shape),
        cost_estimate=pl.CostEstimate(
            flops=count * 100_000_000, bytes_accessed=count * 400_000, transcendentals=0
        ),
        compiler_params=pltpu.CompilerParams(vmem_limit_bytes=8 << 20),
        name="spectra",
    )(base, *stretches)


def last_spectra(to_ref, place, row, table, lower, upper):
    rows = table.shape[1]
    phase = jnp.concatenate([lower[...], upper[: rows - lower.shape[0], :]], axis=0)
    out = jnp.dot(table, phase, preferred_element_type=jnp.float32)
    for tile in range(out.shape[1] // LANES):
        to_ref[place + tile, row:, :] = out[:, tile * LANES : (tile + 1) * LANES]


def assemble_kernel(groups, snaps, base_ref, *refs):
    early = refs[: 2 * groups]
    lower, upper, spectra_ref = refs[2 * groups :]
    side = lax.axis_index("gy")
    half = spectra_ref.shape[0] // 2
    each = base_ref.shape[0] // 2
    rows = lower.shape[0] + upper.shape[0] - 8
    done = 0
    for n, ref in enumerate(early):
        side_of = side if n % 2 == 0 else 1 - side
        for tile in range(half):
            spectra_ref[side_of * half + tile, done : done + ref.shape[1], :] = ref[tile]
        done += ref.shape[1] * (n % 2)
    table = shifted_table(base_ref[:each, :], starts_in(upper[rows - lower.shape[0] :, :], snaps))[:, :rows]
    last_spectra(spectra_ref, side * half, done, table, lower, upper)


def assemble(count, snaps, base, early, own):
    half = early[0].shape[0]
    total = count * snaps * base.shape[0] // 2
    vmem = pl.BlockSpec(memory_space=pltpu.VMEM)
    return pl.pallas_call(
        functools.partial(assemble_kernel, len(early) // 2, snaps),
        in_specs=[vmem] * (1 + len(early) + 2),
        out_specs=vmem,
        out_shape=jax.ShapeDtypeStruct((2 * half, total, LANES), jnp.float32),
        compiler_params=pltpu.CompilerParams(vmem_limit_bytes=8 << 20),
        name="assemble",
    )(base, *early, *own)


def gram_kernel(
    snaps, scale, slots, meta_ref, base_ref, extra_ref, lower, upper, given_ref, out_ref, spectra_ref, *rest
):
    *operands, buf_ref, sems = rest
    side = lax.axis_index("gy")
    bins = out_ref.shape[1]
    tiles, total, _ = spectra_ref.shape
    half = tiles // 2
    blocks = tiles * LANES // BLOCK
    each = 2 * bins
    many = total // each
    rows = lower.shape[0] + upper.shape[0] - 8
    extra = extra_ref[rows - lower.shape[0] :, :]
    table = shifted_table(base_ref[:each, :], starts_in(extra, snaps))[:, :rows]
    last_spectra(spectra_ref, (1 - side) * half, total - snaps * each, table, lower, upper)

    def copies(f, slot):
        return [
            pltpu.make_async_copy(buf_ref.at[slot, part, blk], out_ref.at[part, f, blk], sems.at[slot, part, blk])
            for blk in range(blocks)
            for part in range(2)
        ]

    def strain_spectra(row):
        held = [spectra_ref[tile, pl.ds(row, many, stride=each), :] for tile in range(tiles)]
        held.append(jnp.broadcast_to(held[-1][:, LANES - 1 :], held[-1].shape))
        per_block = BLOCK // LANES
        span = BLOCK + LANES
        for blk in range(blocks):
            wide = jnp.concatenate(held[blk * per_block : (blk + 1) * per_block + 1], axis=1)
            moved = pltpu.roll(wide, span - meta_ref[blk], 1)[:, :BLOCK]
            yield (moved - wide[:, :BLOCK]).astype(jnp.bfloat16)

    def prepare(f, to_ref):
        for blk, (real, imag) in enumerate(zip(strain_spectra(f), strain_spectra(bins + f), strict=True)):
            to_ref[blk, :many, :BLOCK] = real
            to_ref[blk, many:, :BLOCK] = imag
            to_ref[blk, :many, BLOCK:] = imag
            to_ref[blk, many:, BLOCK:] = -real

    def multiply(f, from_ref):
        slot = lax.rem(f, slots)
        for blk in range(blocks):
            left = from_ref[blk, :, :BLOCK]
            for k in range(PARTNERS):
                tile = lax.dot_general(
                    left,
                    from_ref[meta_ref[blocks * (1 + k) + blk]],
                    (((0,), (0,)), ((), ())),
                    preferred_element_type=jnp.float32,
                )
                if scale != 1.0:
                    tile = tile * scale
                buf_ref[slot, 0, blk, k] = tile[:, :BLOCK].astype(jnp.bfloat16)
                buf_ref[slot, 1, blk, k] = tile[:, BLOCK:].astype(jnp.bfloat16)
            for c in copies(f, slot)[2 * blk : 2 * blk + 2]:
                c.start()

    def free(f):
        @pl.when(f >= slots)
        def _():
            for n in (f, f + 1):
                for c in copies(n - slots, lax.rem(n, slots)):
                    c.wait()

    def step(i, carry):
        f = 4 * i
        for n in (0, 2):
            free(f + n)
            multiply(f + n, operands[n])
            prepare(lax.rem(f + n + 2, bins), operands[2 - n])
            multiply(f + n + 1, operands[n + 1])
            prepare(lax.rem(f + n + 3, bins), operands[3 - n])
        return carry

    prepare(0, operands[0])
    prepare(1, operands[1])
    lax.fori_loop(0, bins // 4, step, 0)
    for f in range(bins - slots, bins):
        for c in copies(f, f % slots):
            c.wait()


def gram(snaps, scale, meta, base, spectra, extra, sib):
    tiles, total, _ = spectra.shape
    bins = base.shape[0] // 4
    blocks = tiles * LANES // BLOCK
    many = total // (2 * bins)
    slots = 4
    vmem, smem = pl.BlockSpec(memory_space=pltpu.VMEM), pl.BlockSpec(memory_space=pltpu.SMEM)
    out, _ = pl.pallas_call(
        functools.partial(gram_kernel, snaps, scale, slots),
        in_specs=[smem] + [vmem] * 5,
        out_specs=(pl.BlockSpec(memory_space=pltpu.HBM), vmem),
        out_shape=(
            jax.ShapeDtypeStruct((2, bins, blocks, PARTNERS, BLOCK, BLOCK), jnp.bfloat16),
            jax.ShapeDtypeStruct(spectra.shape, spectra.dtype),
        ),
        input_output_aliases={5: 1},
        scratch_shapes=[
            *[pltpu.VMEM((blocks, 2 * many, 2 * BLOCK), jnp.bfloat16)] * 4,
            pltpu.VMEM((slots, 2, blocks, PARTNERS, BLOCK, BLOCK), jnp.bfloat16),
            pltpu.SemaphoreType.DMA((slots, 2, blocks)),
        ],
        compiler_params=pltpu.CompilerParams(vmem_limit_bytes=24 << 20),
        name="gram",
    )(meta, base, extra, *sib, spectra)
    return out


def on_device_ring(optical_phase, gauge_length, snap_starts, partner_offsets):
    count = lax.axis_size("gx")
    pair_devices = lax.axis_size("gy")
    rows_local = optical_phase.shape[0]
    bins_dev = BINS // (count * pair_devices)
    snaps = snap_starts.shape[0]
    order = ring_order(count)

    scale = 1.0 / math.sqrt(count * snaps)
    root = math.sqrt(scale)
    if math.frexp(root)[0] == 0.5:
        fold, scale = root, 1.0
    else:
        fold = 1.0

    cores = lax.axis_index("gy") ^ jnp.arange(pair_devices, dtype=jnp.int32)
    first_bin = (lax.axis_index("gx") * pair_devices + cores) * bins_dev
    bin_index = (first_bin[:, None] + jnp.arange(bins_dev, dtype=jnp.int32)[None, :]).reshape(-1)
    fourier = fourier_table(bin_index, 2 * BINS).astype(jnp.float32) * (taper_window() * fold)
    base = fourier.astype(jnp.bfloat16).astype(jnp.float32).reshape(2, pair_devices, bins_dev, SNAP_LEN)
    base = jnp.transpose(base, (1, 0, 2, 3)).reshape(2 * pair_devices * bins_dev, SNAP_LEN)
    base = jnp.pad(base, ((0, 0), (0, SNAP_LEN)))

    def exchange(x):
        return lax.ppermute(x, "gy", [(0, 1), (1, 0)])

    def tie(*xs):
        return lax.optimization_barrier(xs)

    def spectra(*stretches):
        return spectra_group(snaps, base, stretches)

    def moved(x, places):
        return lax.ppermute(x, "gx", [(order[i], order[(i + places) % count]) for i in range(count)])

    def onward(f, b, places=1):
        f = moved(f, places)
        b = moved(b, -places)
        return f, b

    lead_rows = rows_local * 3 // 5 // 16 * 16
    half = optical_phase.shape[1]
    extra = snap_starts.astype(optical_phase.dtype)[:, None, None]
    extra = jnp.broadcast_to(extra, (snaps, 8 // snaps, half)).reshape(8, half)
    f1, b1 = onward(optical_phase, optical_phase)
    ef, eb = onward(extra, extra)
    f1, b1 = jnp.concatenate([f1, ef]), jnp.concatenate([b1, eb])
    own = jnp.concatenate([optical_phase, extra])
    f2, b2 = onward(f1, b1)
    near1, far1 = spectra(own, f1, b1)
    near1, gauges, offsets = tie(near1, gauge_length, partner_offsets)
    partners = offsets.T + jnp.arange(offsets.shape[0], dtype=jnp.int32)[None, :]
    meta = jnp.concatenate([gauges, partners.reshape(-1)])
    other1 = exchange(far1)
    f3, b3 = onward(f2, b2)
    f4, b4 = onward(f2[:lead_rows], b2[lead_rows:], 2)
    near2, far2 = spectra(f2, b2)
    other2 = exchange(far2)
    b4, meta = tie(b4, meta)
    near3, far3 = spectra(f3, b3)
    s_b4 = exchange(b4)
    s_f4 = exchange(f4)
    other3 = exchange(far3)
    early = (near1, other1, near2, other2, near3, other3)
    joined = assemble(count, snaps, base, early, (f4, b4))
    return gram(snaps, scale, meta, base, joined, b4, (s_f4, s_b4))


def strain_blocks(extended, gauges):
    blocks = gauges.shape[0]
    block_first = jnp.arange(blocks, dtype=jnp.int32) * BLOCK

    def pick_block(column):
        return lax.dynamic_slice_in_dim(extended, column, BLOCK, 1)

    shifted = jax.vmap(pick_block)(block_first + gauges)
    initial = extended[:, : blocks * BLOCK].reshape(extended.shape[0], blocks, BLOCK)
    return shifted - jnp.transpose(initial, (1, 0, 2))


def tapered_segments(strain, start_rows):
    window = taper_window()

    def segment_at(row_start):
        return lax.dynamic_slice_in_dim(strain, row_start, SNAP_LEN, 1)

    segments = jax.vmap(segment_at)(start_rows)
    return (window[None, None, :, None] * segments).astype(jnp.bfloat16)


def spectra_for(tapered, bin_index):
    fourier = fourier_table(bin_index, 2 * BINS)
    spectrum = jnp.einsum("cft,sbtj->scfbj", fourier, tapered, preferred_element_type=jnp.float32)
    shape_out = spectrum.shape
    return spectrum.astype(jnp.bfloat16).reshape(
        shape_out[0], 2, shape_out[2], shape_out[3] * BLOCK
    )


def on_device(optical_phase, gauge_length, snap_starts, partner_offsets):
    time_devices = lax.axis_size("gx")
    pair_devices = lax.axis_size("gy")
    pair_index = lax.axis_index("gy")
    rows_local = optical_phase.shape[0]
    bins_dev = BINS // (time_devices * pair_devices)
    whole_phase = lax.all_gather(optical_phase, "gy", axis=1, tiled=True)
    edge_cols = jnp.broadcast_to(whole_phase[:, -1:], (rows_local, GAUGE_MAX))
    extended = jnp.concatenate([whole_phase, edge_cols], axis=1).astype(jnp.float32)
    strain = strain_blocks(extended, gauge_length)
    tapered = tapered_segments(strain, snap_starts)
    owner_slot = jnp.arange(time_devices * bins_dev, dtype=jnp.int32)
    bin_index = (
        owner_slot // bins_dev * pair_devices + pair_index
    ) * bins_dev + owner_slot % bins_dev
    spectra = spectra_for(tapered, bin_index)
    gathered = lax.all_to_all(spectra, "gx", split_axis=2, concat_axis=0, tiled=True)
    snaps_all = gathered.shape[0]
    blocks_all = gathered.shape[3] // BLOCK
    spectra_blocks = gathered.reshape(snaps_all, 2, bins_dev, blocks_all, BLOCK)
    partners = jnp.arange(blocks_all, dtype=jnp.int32)[:, None] + partner_offsets
    partner_data = jnp.take(spectra_blocks, partners.reshape(-1), axis=3)
    partner_data = partner_data.reshape(snaps_all, 2, bins_dev, blocks_all, PARTNERS, BLOCK)
    swapped = jnp.stack([partner_data[:, 1], -partner_data[:, 0]], axis=1)
    stacked = jnp.stack([partner_data, swapped])
    gram_tile = jnp.einsum(
        "scfbi,pscfbkj->pfbkij", spectra_blocks, stacked, preferred_element_type=jnp.float32
    )
    return (gram_tile * (1.0 / math.sqrt(snaps_all))).astype(jnp.bfloat16)


def solution(mesh):
    in_specs = (P(("fiber", "gx"), "gy"), P("fiber"), P(("fiber", "gx")), P("fiber", None))
    out_specs = P("fiber", ("gx", "gy"), None, None, None, None)

    def body(optical_phase, gauge_length, snap_starts, partner_offsets):
        ring = lax.axis_size("gx") == 8 and lax.axis_size("gy") == 2 and snap_starts.shape[0] == 2
        plan = on_device_ring if ring else on_device
        return plan(optical_phase, gauge_length, snap_starts, partner_offsets)

    return jax.shard_map(body, mesh=mesh, in_specs=in_specs, out_specs=out_specs, check_vma=False)
```
